32 devices in a mesh: subj: 2 (over y), band: 4 (over z), lon: 2 (over x), pop: 2 (over core).
Axes of the slice: x: 2, y: 2, z: 4, core: 2. Of those that a mesh axis runs over, the one named last changes fastest.
Arguments:
- activity: float32 [16, 640, 1280], P(('subj', 'pop'), 'band', 'lon'), parts along dimension 0, may hold values from -6 to 6
- drive: bfloat16 [16, 640, 1280], P(('subj', 'pop'), 'band', 'lon'), parts along dimension 0, may hold values from -6 to 6
- basis: bfloat16 [1280, 320, 640], P(('subj', 'band', 'lon')), parts along dimension 0, may hold values from -6 to 6
- kernels: float32 [4, 640], replicated, may hold values from 0.2 to 2
- conn_block: int32 [8, 8], replicated, may hold values from 0 to 3
- coupling: float32 [16, 8], P('subj'), parts along dimension 0, may hold values from -2.5 to 2.5
- rate_params: float32 [8, 8], P('subj'), parts along dimension 0, may hold values from 0.5 to 2
Outputs:
- activity_next: float32 [16, 640, 1280], P(('subj', 'pop'), 'band', 'lon'), parts along dimension 0
The draws below stay inside these ranges and needn't reach their ends.
There are 2 independent parts, one for each index of `subj`. The reference program is written for one: setup_inputs(seed, part) draws one part's arguments, and reference() takes and returns one part's arrays. A program takes and returns all parts, laid end to end along the dimension named above; an argument that names none is the same for every part. Nothing has to cross between parts.
All inputs are finite; a program needn't handle non-finite values.
Results may differ from the reference program's by a relative error of at most 0.0095.
Values may be sent and summed in bfloat16 or wider, within the bound.
A program may use at most 192 MiB of HBM per device.

```python
import math
import jax
import jax.numpy as jnp
from jax import lax

POP = 8
NK = 4
NLAT = 640
NLON = 1280
DEG = 640
STEPS = 2


def place_ends(values, key, least, top_value):
    dims = values.shape
    index_at = [jax.random.randint(jax.random.fold_in(key, axis), (), 0, dims[axis]) for axis in range(len(dims))]
    values = values.at[tuple(index_at)].set(least)
    longest = dims.index(max(dims))
    index_at[longest] = (index_at[longest] + 1) % dims[longest]
    return values.at[tuple(index_at)].set(top_value)


def levels(key, shape, cuts, least, high):
    level = 1.0
    for dim, blocks in cuts:
        heights = jax.random.uniform(jax.random.fold_in(jax.random.fold_in(key, 6), dim), (blocks,), jnp.float32, least / len(cuts), high / len(cuts))
        level = level * jnp.repeat(jnp.exp(heights), shape[dim] // blocks).reshape((-1,) + (1,) * (len(shape) - 1 - dim))
    return level


def noise(rng, shape, spread, bound, cuts=(), kind=jnp.bfloat16):
    array = spread * jax.random.normal(rng, shape, jnp.float32)
    if cuts:
        array = array * levels(rng, shape, cuts, -0.22, 0.18)
    return jnp.clip(array, -bound, bound).astype(kind)


def setup_inputs(seed: int = 0, part: int = 0) -> dict:
    splits = jax.random.split(jax.random.key(seed), 8)
    part_splits = jax.random.split(jax.random.fold_in(splits[7], part), 8)
    activity = noise(part_splits[0], (POP, NLAT, NLON), 1.0, 6.0, ((0, 2), (1, 4), (2, 2)), jnp.float32)
    drive = noise(part_splits[1], (POP, NLAT, NLON), 1.0, 6.0, ((0, 2), (1, 4), (2, 2)))
    basis = noise(part_splits[2], (DEG, NLAT // 2, DEG), 1.0, 6.0, ((0, 8),))
    kernels = jnp.clip(jnp.exp(jax.random.uniform(splits[3], (NK, DEG), jnp.float32, math.log(0.2), math.log(2.0))), 0.2, 2.0)
    conn_block = place_ends(jax.random.randint(splits[4], (POP, POP), 0, NK), jax.random.fold_in(splits[4], 1), 0, NK - 1).astype(jnp.int32)
    coupling = noise(part_splits[5], (POP, POP), 0.35, 2.5, (), jnp.float32)
    rate_params = jnp.clip(jax.random.uniform(part_splits[6], (4, POP), jnp.float32, 0.5, 2.0), 0.5, 2.0)
    return {"activity": activity, "drive": drive, "basis": basis, "kernels": kernels, "conn_block": conn_block, "coupling": coupling, "rate_params": rate_params}


time_step = 0.5


def fourier_table():
    longitude = jnp.arange(NLON, dtype=jnp.int32)
    wavenumber = jnp.arange(DEG, dtype=jnp.int32)
    phase = (longitude[:, None] * wavenumber[None, :]) % NLON
    angle = phase.astype(jnp.float32) * (2.0 * math.pi / NLON)
    return jnp.stack([jnp.cos(angle), jnp.sin(angle)], axis=1).astype(jnp.bfloat16)


def lat_weights():
    row_index = jnp.arange(NLAT // 2, dtype=jnp.float32)
    colatitude = math.pi * (4.0 * row_index + 3.0) / (4.0 * NLAT + 2.0)
    return math.pi * jnp.sin(colatitude) / NLAT


def round_trip(values):
    return lax.optimization_barrier(values.astype(jnp.bfloat16)).astype(jnp.float32)


def reference(activity, drive, basis, kernels, conn_block, coupling, rate_params):
    highest = lax.Precision.HIGHEST
    cos_sin = fourier_table().astype(jnp.float32)
    weights = lat_weights()
    half_lat = NLAT // 2
    quarter = DEG // 2
    gain_row, thresh, decay_row, lateral = rate_params[0], rate_params[1], rate_params[2], rate_params[3]
    onehot = (conn_block[..., None] == jnp.arange(kernels.shape[0], dtype=jnp.int32)).astype(jnp.float32)
    mixing = coupling[..., None] * jnp.einsum('ijb,bn->ijn', onehot, kernels, precision=highest)
    wavenumber = jnp.arange(DEG, dtype=jnp.int32)
    degree = jnp.arange(DEG, dtype=jnp.int32)
    amplitude = jnp.where(wavenumber == 0, 1.0, 2.0).astype(jnp.float32)
    slots = jnp.arange(2, dtype=jnp.int32)

    def analyse(block_item):
        spectrum, basis_block, wavenum = block_item
        northern = spectrum[..., :half_lat]
        southern = jnp.flip(spectrum[..., half_lat:], axis=-1)
        even_part = round_trip(weights * (northern + southern))
        odd_part = round_trip(weights * (northern - southern))
        parity_pick = slots == wavenum % 2
        operand = jnp.where(parity_pick[None, None, :, None], even_part[:, :, None, :], odd_part[:, :, None, :])
        basis_split = basis_block.astype(jnp.float32).reshape(half_lat, quarter, 2)
        coefficients = jnp.einsum('icsj,jqs->icqs', operand, basis_split, precision=highest)
        coefficients = coefficients.reshape(POP, 2, DEG)
        return jnp.where(degree >= wavenum, coefficients, 0.0)

    def synthesise(block_item):
        spectrum, basis_block, wavenum = block_item
        basis_split = basis_block.astype(jnp.float32).reshape(half_lat, quarter, 2)
        degree_parts = jnp.einsum('icqs,jqs->icsj', spectrum.reshape(POP, 2, quarter, 2), basis_split, precision=highest)
        parity_pick = (slots == wavenum % 2)[None, None, :, None]
        same_parity = jnp.sum(jnp.where(parity_pick, degree_parts, 0.0), axis=2)
        other_parity = jnp.sum(jnp.where(parity_pick, 0.0, degree_parts), axis=2)
        joined = jnp.concatenate([same_parity + other_parity, jnp.flip(same_parity - other_parity, axis=-1)], axis=-1)
        return joined.astype(jnp.bfloat16)

    activity_now = activity
    for step_index in range(STEPS):
        rates = jax.nn.sigmoid(gain_row[:, None, None] * (activity_now - thresh[:, None, None]))
        rates_f32 = round_trip(rates)
        fourier = jnp.einsum('ijk,kcm->micj', rates_f32, cos_sin, precision=highest)
        fourier = round_trip(fourier)
        coeffs = lax.map(analyse, (fourier, basis, wavenumber))
        mixed_spec = jnp.einsum('ijn,mjcn->micn', mixing, coeffs, precision=highest)
        mixed_spec = round_trip(mixed_spec)
        synthesis = lax.map(synthesise, (mixed_spec, basis, wavenumber))
        scaled = synthesis.astype(jnp.float32) * amplitude[:, None, None, None]
        synth_field = jnp.einsum('micj,kcm->ijk', scaled, cos_sin, precision=highest) / NLON
        padded = jnp.pad(rates_f32, ((0, 0), (1, 1), (0, 0)))
        lateral_term = (jnp.roll(rates_f32, 1, axis=2) + jnp.roll(rates_f32, -1, axis=2)
                        + padded[:, 2:, :] + padded[:, :-2, :] - 4.0 * rates_f32)
        forcing = (-decay_row[:, None, None] * activity_now + synth_field
                   + lateral[:, None, None] * lateral_term + drive.astype(jnp.float32))
        activity_now = activity_now + time_step * forcing
    return activity_now
```

```python
import functools
import math

import jax
import jax.numpy as jnp
from jax import lax
from jax.experimental import pallas as pl
from jax.experimental.pallas import tpu as pltpu
from jax.sharding import PartitionSpec as P

NLAT = 640
NLON = 1280
DEG = 640
STEPS = 2


time_step = 0.5


def with_halo(shard, sides, width):
    for axis, dim in sides:
        size, length = (lax.axis_size(axis), shard.shape[dim])
        up = [(i, (i + 1) % size) for i in range(size - 1)]
        down = [(j, i) for i, j in up]
        last = lax.slice_in_dim(shard, length - width, length, axis=dim)
        leading = lax.slice_in_dim(shard, 0, width, axis=dim)
        before = lax.ppermute(last, axis, up)
        after = lax.ppermute(leading, axis, down)
        shard = jnp.concatenate([before, shard, after], axis=dim)
    return shard


def fourier_table():
    longitude = jnp.arange(NLON, dtype=jnp.int32)
    wavenumber = jnp.arange(DEG, dtype=jnp.int32)
    phase = longitude[:, None] * wavenumber[None, :] % NLON
    angle = phase.astype(jnp.float32) * (2.0 * math.pi / NLON)
    return jnp.stack([jnp.cos(angle), jnp.sin(angle)], axis=1).astype(jnp.bfloat16)


def lat_weights():
    row_index = jnp.arange(NLAT // 2, dtype=jnp.float32)
    colatitude = math.pi * (4.0 * row_index + 3.0) / (4.0 * NLAT + 2.0)
    return math.pi * jnp.sin(colatitude) / NLAT


def to_owners(fourier):
    return lax.all_to_all(fourier, ("band", "lon"), split_axis=2, concat_axis=3, tiled=True)


def to_latitudes(synthesis):
    return lax.all_to_all(synthesis, ("band", "lon"), split_axis=3, concat_axis=2, tiled=True)


def local(activity, drive, basis, kernels, conn_block, coupling, rate_params):
    pop_here = activity.shape[0]
    owned_count = basis.shape[0]
    half_lat = basis.shape[1]
    quarter = DEG // 2
    owner_index = lax.axis_index("band") * lax.axis_size("lon") + lax.axis_index("lon")
    pop_first = lax.axis_index("pop") * pop_here
    params = lax.dynamic_slice_in_dim(rate_params, pop_first, pop_here, 1)
    gain_row, thresh, decay_row, lateral = (params[0], params[1], params[2], params[3])
    cos_sin = fourier_table()
    weights = lat_weights()
    wavenumber = owner_index * owned_count + jnp.arange(owned_count, dtype=jnp.int32)
    degree = jnp.arange(DEG, dtype=jnp.int32)
    triangle = degree[None, :] >= wavenumber[:, None]
    slots = jnp.arange(2, dtype=jnp.int32)
    parity_pick = (slots[None, :] == (wavenumber % 2)[:, None])[None, None, :, :, None]
    every_wave = jnp.arange(DEG, dtype=jnp.int32)
    amplitude = jnp.where(every_wave == 0, 1.0, 2.0).astype(jnp.bfloat16)
    coup_own = lax.dynamic_slice_in_dim(coupling, pop_first, pop_here, 0)
    block_own = lax.dynamic_slice_in_dim(conn_block, pop_first, pop_here, 0)
    onehot = (block_own[..., None] == jnp.arange(kernels.shape[0], dtype=jnp.int32)).astype(
        jnp.float32
    )
    mixing = coup_own[..., None] * jnp.einsum(
        "ijb,bn->ijn", onehot, kernels, precision=lax.Precision.HIGHEST
    )
    basis_split = basis.reshape(owned_count, half_lat, quarter, 2)
    drive_f32 = drive.astype(jnp.float32)
    activity_now = activity
    for step_index in range(STEPS):
        rates = jax.nn.sigmoid(
            gain_row[:, None, None] * (activity_now - thresh[:, None, None])
        ).astype(jnp.bfloat16)
        lat_rows = lax.all_to_all(rates, "lon", split_axis=1, concat_axis=2, tiled=True)
        fourier = jnp.einsum(
            "ijk,kcm->icmj", lat_rows, cos_sin, preferred_element_type=jnp.float32
        ).astype(jnp.bfloat16)
        spectrum = to_owners(fourier)
        northern = spectrum[..., :half_lat].astype(jnp.float32)
        southern = jnp.flip(spectrum[..., half_lat:], axis=3).astype(jnp.float32)
        even_part = (weights * (northern + southern)).astype(jnp.bfloat16)
        odd_part = (weights * (northern - southern)).astype(jnp.bfloat16)
        operand = jnp.where(parity_pick, even_part[:, :, :, None, :], odd_part[:, :, :, None, :])
        coeffs = jnp.einsum(
            "icmsj,mjqs->icmqs", operand, basis_split, preferred_element_type=jnp.float32
        )
        coeffs = coeffs.reshape(pop_here, 2, owned_count, DEG)
        coeffs = jnp.where(triangle[None, None], coeffs, 0.0)
        gathered = lax.all_gather(coeffs.astype(jnp.bfloat16), "pop", axis=0, tiled=True).astype(
            coeffs.dtype
        )
        mixed_spec = jnp.sum(mixing[:, :, None, None, :] * gathered[None], axis=1).astype(
            jnp.bfloat16
        )
        degree_parts = jnp.einsum(
            "icmqs,mjqs->icmsj",
            mixed_spec.reshape(pop_here, 2, owned_count, quarter, 2),
            basis_split,
            preferred_element_type=jnp.float32,
        )
        same_parity = jnp.sum(jnp.where(parity_pick, degree_parts, 0.0), axis=3)
        other_parity = jnp.sum(jnp.where(parity_pick, 0.0, degree_parts), axis=3)
        synthesis = jnp.concatenate(
            [same_parity + other_parity, jnp.flip(same_parity - other_parity, axis=3)], axis=3
        ).astype(jnp.bfloat16)
        returned = to_latitudes(synthesis)
        scaled = returned * amplitude[None, None, :, None]
        synth_field = jnp.einsum(
            "icmj,kcm->ijk", scaled, cos_sin, preferred_element_type=jnp.float32
        ) * (1.0 / NLON)
        padded = with_halo(lat_rows, ((("band", "lon"), 1),), 1).astype(jnp.float32)
        rates_f32 = lat_rows.astype(jnp.float32)
        lateral_term = (
            jnp.roll(rates_f32, 1, axis=2)
            + jnp.roll(rates_f32, -1, axis=2)
            + padded[:, 2:, :]
            + padded[:, :-2, :]
            - 4.0 * rates_f32
        )
        coupled = synth_field + lateral[:, None, None] * lateral_term
        coupled_grid = lax.all_to_all(
            coupled.astype(jnp.bfloat16), "lon", split_axis=2, concat_axis=1, tiled=True
        ).astype(coupled.dtype)
        forcing = -decay_row[:, None, None] * activity_now + coupled_grid + drive_f32
        activity_now = activity_now + time_step * forcing
    return activity_now


MESH = pl.DeviceIdType.MESH
LANES = 128


def greet(nband):
    band, lon = lax.axis_index("band"), lax.axis_index("lon")
    barrier = pltpu.get_barrier_semaphore()
    for d in range(1, nband):
        peer = {"band": lax.rem(band + d, nband)}
        pl.semaphore_signal(barrier, inc=1, device_id=peer, device_id_type=MESH)
    pl.semaphore_signal(barrier, inc=1, device_id={"lon": 1 - lon}, device_id_type=MESH)
    pl.semaphore_wait(barrier, nband)


def remote(src, dst, send_sem, recv_sem, peer):
    return pltpu.make_async_remote_copy(
        src_ref=src, dst_ref=dst, send_sem=send_sem, recv_sem=recv_sem,
        device_id=peer, device_id_type=MESH,
    )


def forward_kernel(nband, r_ref, t_ref, e_ref, g_ref, rp_ref, eo_ref, f_ref, xs, xr, zs, zr, es, er):
    band, lon = lax.axis_index("band"), lax.axis_index("lon")
    rows, nlon = r_ref.shape
    block = t_ref.shape[0] // nband
    chunks = rows // LANES
    greet(nband)
    copies = []
    arrivals = []
    for q in range(chunks):
        part = pl.ds(q * LANES, LANES)
        copy = remote(r_ref.at[part], rp_ref.at[part], xs.at[q], xr.at[q], {"lon": 1 - lon})
        copy.start()
        arrivals.append(copy)
    for side, step in ((0, 1), (1, nband - 1)):
        peer = {"band": lax.rem(band + step, nband)}
        copy = remote(e_ref.at[side], eo_ref.at[side], es.at[side], er.at[side], peer)
        copy.start()
        copies.append(copy)
    contract = (((1,), (1,)), ((), ()))
    for q in range(chunks):
        part = pl.ds(q * LANES, LANES)
        total = lax.dot_general(
            t_ref[:, :nlon], r_ref[part, :], contract, preferred_element_type=jnp.float32
        )
        arrivals[q].wait_recv()
        total += lax.dot_general(
            t_ref[:, nlon:], rp_ref[part, :], contract, preferred_element_type=jnp.float32
        )
        f_ref[q] = total.astype(f_ref.dtype)
        for d in range(1, nband):
            dest = lax.rem(band + d, nband)
            rows_out = pl.ds(pl.multiple_of(dest * block, 16), block)
            copy = remote(
                f_ref.at[q, rows_out], g_ref.at[band, :, part],
                zs.at[q, d - 1], zr.at[q, d - 1], {"band": dest},
            )
            copy.start()
            copies.append(copy)
        own = pl.ds(pl.multiple_of(band * block, 16), block)
        g_ref[band, :, part] = f_ref[q, own]
    for copy in arrivals:
        copy.wait_send()
    for copy in copies:
        copy.wait()


def forward(rates, table, edges, nband):
    rows, nlon = rates.shape
    width = table.shape[0]
    chunks = rows // LANES
    dma = pltpu.SemaphoreType.DMA
    vmem = pl.BlockSpec(memory_space=pltpu.VMEM)
    return pl.pallas_call(
        functools.partial(forward_kernel, nband),
        out_shape=(
            jax.ShapeDtypeStruct((nband, width // nband, rows), jnp.bfloat16),
            jax.ShapeDtypeStruct((rows, nlon), jnp.bfloat16),
            jax.ShapeDtypeStruct(edges.shape, jnp.bfloat16),
        ),
        in_specs=[vmem] * 3,
        out_specs=(vmem,) * 3,
        scratch_shapes=[
            pltpu.VMEM((chunks, width, LANES), jnp.bfloat16),
            dma((chunks,)), dma((chunks,)),
            dma((chunks, nband - 1)), dma((chunks, nband - 1)),
            dma((2,)), dma((2,)),
        ],
        compiler_params=pltpu.CompilerParams(collective_id=0, has_side_effects=True),
        name="forward_exchange",
    )(rates, table, edges)


def backward_kernel(nband, s_ref, o_ref, zs, zr, xs, xr):
    band, lon = lax.axis_index("band"), lax.axis_index("lon")
    rows = s_ref.shape[2]
    chunks = rows // LANES
    partner = {"lon": 1 - lon}
    greet(nband)
    crossing = []
    for q in range(chunks):
        part = pl.ds(q * LANES, LANES)
        copy = remote(
            s_ref.at[band, :, part], o_ref.at[1, band, :, part], xs.at[q, 0], xr.at[q, 0], partner
        )
        copy.start()
        crossing.append(copy)
    along = []
    for q in range(chunks):
        part = pl.ds(q * LANES, LANES)
        for d in range(1, nband):
            dest = lax.rem(band + d, nband)
            copy = remote(
                s_ref.at[dest, :, part], o_ref.at[0, band, :, part],
                zs.at[q, d - 1], zr.at[q, d - 1], {"band": dest},
            )
            copy.start()
            along.append(copy)
    o_ref[0, band] = s_ref[band]
    for q in range(chunks):
        part = pl.ds(q * LANES, LANES)
        for d in range(1, nband):
            along[q * (nband - 1) + d - 1].wait_recv()
            source = lax.rem(band + nband - d, nband)
            copy = remote(
                o_ref.at[0, source, :, part], o_ref.at[1, source, :, part],
                xs.at[q, d], xr.at[q, d], partner,
            )
            copy.start()
            crossing.append(copy)
    for copy in along:
        copy.wait_send()
    for copy in crossing:
        copy.wait()


def backward(synthesis, nband):
    rows = synthesis.shape[2]
    chunks = rows // LANES
    dma = pltpu.SemaphoreType.DMA
    vmem = pl.BlockSpec(memory_space=pltpu.VMEM)
    return pl.pallas_call(
        functools.partial(backward_kernel, nband),
        out_shape=jax.ShapeDtypeStruct((2,) + synthesis.shape, jnp.bfloat16),
        in_specs=[vmem],
        out_specs=vmem,
        scratch_shapes=[
            dma((chunks, nband - 1)), dma((chunks, nband - 1)),
            dma((chunks, nband)), dma((chunks, nband)),
        ],
        compiler_params=pltpu.CompilerParams(collective_id=1, has_side_effects=True),
        name="backward_exchange",
    )(synthesis)


def spectral_kernel(group, x_ref, b_hbm, a_ref, k_ref, s_ref, b_ref, own_ref, other_ref, bsem, ss, rs):
    owned, _, deg = b_ref.shape
    owner = lax.axis_index("band") * lax.axis_size("lon") + lax.axis_index("lon")
    first = owner * owned
    chunks = owned // group
    kinds = k_ref.shape[0]
    partner = {"pop": 1 - lax.axis_index("pop")}

    def fetch(c):
        part = pl.ds(c * group, group)
        return pltpu.make_async_copy(b_hbm.at[part], b_ref.at[part], bsem.at[c])

    def swap(c):
        part = pl.ds(c * group, group)
        return remote(own_ref.at[part], other_ref.at[part], ss.at[c], rs.at[c], partner)

    @pl.loop(0, chunks)
    def _(c):
        fetch(c).start()

    barrier = pltpu.get_barrier_semaphore()
    pl.semaphore_signal(barrier, inc=1, device_id=partner, device_id_type=MESH)
    pl.semaphore_wait(barrier, 1)
    degree = lax.broadcasted_iota(jnp.int32, (own_ref.shape[1], deg), 1)
    half = own_ref.shape[1]

    @pl.loop(0, chunks)
    def _(c):
        fetch(c).wait()
        for g in range(group):
            m = c * group + g
            both = jnp.dot(x_ref[m], b_ref[m], preferred_element_type=jnp.float32)
            gap = degree - (first + m)
            coeffs = jnp.where(gap % 2 == 0, both[:half], both[half:])
            own_ref[m] = jnp.where(gap >= 0, coeffs, 0.0).astype(own_ref.dtype)
        swap(c).start()

    @pl.loop(0, chunks)
    def _(c):
        swap(c).wait_recv()
        for g in range(group):
            m = c * group + g
            pair = jnp.concatenate(
                [own_ref[m].astype(jnp.float32), other_ref[m].astype(jnp.float32)], axis=0
            ).astype(jnp.bfloat16)
            by_kind = jnp.dot(
                a_ref[...], jnp.concatenate([pair, pair], axis=0),
                preferred_element_type=jnp.float32,
            )
            mixed = k_ref[0:1] * by_kind[:half]
            for kind in range(1, kinds):
                mixed += k_ref[kind : kind + 1] * by_kind[kind * half : (kind + 1) * half]
            gap = degree - (first + m)
            signed = jnp.where(gap % 2 == 0, mixed, -mixed)
            s_ref[m] = lax.dot_general(
                jnp.concatenate([mixed, signed], axis=0).astype(jnp.bfloat16), b_ref[m],
                (((1,), (1,)), ((), ())), preferred_element_type=jnp.float32,
            ).astype(s_ref.dtype)

    @pl.loop(0, chunks)
    def _(c):
        swap(c).wait_send()


def spectral(operand, basis, by_kind, kernels):
    owned, half_lat, deg = basis.shape
    both = operand.shape[1]
    group = 8
    chunks = owned // group
    dma = pltpu.SemaphoreType.DMA
    vmem = pl.BlockSpec(memory_space=pltpu.VMEM)
    return pl.pallas_call(
        functools.partial(spectral_kernel, group),
        out_shape=jax.ShapeDtypeStruct(operand.shape, jnp.bfloat16),
        in_specs=[vmem, pl.BlockSpec(memory_space=pltpu.MemorySpace.HBM), vmem, vmem],
        out_specs=vmem,
        scratch_shapes=[
            pltpu.VMEM(basis.shape, jnp.bfloat16),
            pltpu.VMEM((owned, both // 2, deg), jnp.bfloat16),
            pltpu.VMEM((owned, both // 2, deg), jnp.bfloat16),
            dma((chunks,)), dma((chunks,)), dma((chunks,)),
        ],
        compiler_params=pltpu.CompilerParams(
            collective_id=2, has_side_effects=True, vmem_limit_bytes=56 * 2**20
        ),
        name="spectral_mix",
    )(operand, basis, by_kind, kernels)


def wave_table(starts, owned, longitude, period):
    coarse = starts[:, None] + 16 * jnp.arange(owned // 16, dtype=jnp.int32)[None, :]
    fine = jnp.arange(16, dtype=jnp.int32)

    def angles(wave):
        phase = wave[..., None] * longitude % period
        angle = phase.astype(jnp.float32) * (2.0 * math.pi / period)
        return lax.optimization_barrier((jnp.cos(angle), jnp.sin(angle)))

    cos_a, sin_a = (v[:, :, None, :] for v in angles(coarse))
    cos_b, sin_b = (v[None, None, :, :] for v in angles(fine))
    shape = (starts.shape[0], owned, longitude.shape[0])
    cosine = (cos_a * cos_b - sin_a * sin_b).reshape(shape)
    sine = (sin_a * cos_b + cos_a * sin_b).reshape(shape)
    return jnp.stack([cosine, sine], axis=1)


def fast_local(activity, drive, basis, kernels, conn_block, coupling, rate_params):
    npop, nlat, nlon = activity.shape
    owned, half_lat, deg = basis.shape
    nband = lax.axis_size("band")
    hb = nband // 2
    period = nlon * lax.axis_size("lon")
    rows = npop * nlat
    band, lon, pop = lax.axis_index("band"), lax.axis_index("lon"), lax.axis_index("pop")
    pop_first = pop * npop
    params = lax.dynamic_slice_in_dim(rate_params, pop_first, npop, 1)[:, :, None, None]
    gain_row, thresh, decay_row, lateral = (params[0], params[1], params[2], params[3])

    bands = jnp.arange(nband, dtype=jnp.int32)
    kk = jnp.arange(nlon, dtype=jnp.int32)
    own_start = (bands * 2 + lon) * owned
    other_start = (bands * 2 + 1 - lon) * owned
    k_order = jnp.concatenate([lon * nlon + kk, (1 - lon) * nlon + kk])
    analysis_table = (
        wave_table(own_start, owned, k_order, period).reshape(deg, period).astype(jnp.bfloat16)
    )
    starts = jnp.concatenate([own_start, other_start])
    waves = starts[:, None] + jnp.arange(owned, dtype=jnp.int32)[None, :]
    amplitude = jnp.where(waves == 0, 1.0, 2.0)[:, None, :, None]
    synthesis_table = (
        (wave_table(starts, owned, lon * nlon + kk, period) * amplitude)
        .reshape(2 * deg, nlon)
        .astype(jnp.bfloat16)
    )

    row_index = jnp.arange(half_lat, dtype=jnp.float32)
    colatitude = math.pi * (4.0 * row_index + 3.0) / (8.0 * half_lat + 2.0)
    weights = math.pi * jnp.sin(colatitude) / (2.0 * half_lat)
    weights = weights.reshape(hb, 1, 1, 1, nlat)

    south = band >= hb
    lat = jnp.arange(nlat, dtype=jnp.int32)
    mirror = (lat[:, None] == jnp.where(south, nlat - 1 - lat, lat)[None, :]).astype(jnp.bfloat16)

    coup_own = lax.dynamic_slice_in_dim(coupling, pop_first, npop, 0)
    block_own = lax.dynamic_slice_in_dim(conn_block, pop_first, npop, 0)
    kind = jnp.arange(kernels.shape[0], dtype=jnp.int32)
    per_kind = jnp.where(block_own[None] == kind[:, None, None], coup_own[None], 0.0)
    per_kind = jnp.concatenate(
        [
            lax.dynamic_slice_in_dim(per_kind, pop_first, npop, 2),
            lax.dynamic_slice_in_dim(per_kind, (1 - pop) * npop, npop, 2),
        ],
        axis=2,
    )
    spread = per_kind[:, :, None, :, None] * jnp.eye(2, dtype=jnp.float32)[:, None, :]
    spread = spread.reshape(kernels.shape[0] * npop * 2, 2 * npop * 2)
    coarse = lax.reduce_precision(spread, 8, 7)
    by_kind = jnp.concatenate([coarse, spread - coarse], axis=1).astype(jnp.bfloat16)

    drive_f32 = drive.astype(jnp.float32)
    u = activity
    for step_index in range(STEPS):
        rates = jax.nn.sigmoid(gain_row * (u - thresh)).astype(jnp.bfloat16)
        facing = jnp.einsum(
            "aj,ijk->iak", mirror, rates, preferred_element_type=jnp.float32
        ).astype(jnp.bfloat16)
        edges = jnp.stack([rates[:, nlat - 1, :], rates[:, 0, :]])
        edges = jnp.pad(edges, ((0, 0), (0, 16 - npop), (0, 0)))
        spectrum, partner, around = forward(
            facing.reshape(rows, nlon), analysis_table, edges, nband
        )
        spectrum = spectrum.reshape(nband, 2, owned, npop, nlat).astype(jnp.float32)
        northern = spectrum[:hb]
        southern = jnp.stack([spectrum[nband - 1 - h] for h in range(hb)])
        parts = jnp.stack(
            [
                (weights * (northern + southern)).astype(jnp.bfloat16),
                (weights * (northern - southern)).astype(jnp.bfloat16),
            ]
        )
        operand = parts.transpose(3, 0, 4, 2, 1, 5).reshape(owned, 4 * npop, half_lat)
        fields = spectral(operand, basis, by_kind, kernels)
        fields = fields.reshape(owned, 2, npop, 2, hb, nlat)
        outgoing = jnp.concatenate(
            [fields[:, 0:1], fields[:, 1:2]], axis=1
        ).transpose(1, 4, 3, 0, 2, 5)
        outgoing = jnp.concatenate(
            [outgoing[0]] + [outgoing[1, h : h + 1] for h in reversed(range(hb))]
        ).reshape(nband, 2 * owned, rows)
        returned = backward(outgoing, nband).reshape(2 * deg, npop, nlat)
        returned = jnp.einsum(
            "wij,aj->wia", returned, mirror, preferred_element_type=jnp.float32
        ).astype(jnp.bfloat16)
        synth_field = jnp.einsum(
            "wia,wk->iak", returned, synthesis_table, preferred_element_type=jnp.float32
        ) * (1.0 / period)
        rates_f32 = rates.astype(jnp.float32)
        partner = partner.reshape(npop, nlat, nlon)
        ends = jnp.stack([partner[:, :, nlon - 1], partner[:, :, 0]])
        ends = jnp.where(south, jnp.flip(ends, axis=2), ends).astype(jnp.float32)
        around = around[:, :npop, None, :].astype(jnp.float32)
        above = jnp.where(band > 0, around[0], 0.0)
        below = jnp.where(band < nband - 1, around[1], 0.0)
        lateral_term = (
            jnp.concatenate([ends[0][:, :, None], rates_f32[:, :, :-1]], axis=2)
            + jnp.concatenate([rates_f32[:, :, 1:], ends[1][:, :, None]], axis=2)
            + jnp.concatenate([above, rates_f32[:, :-1, :]], axis=1)
            + jnp.concatenate([rates_f32[:, 1:, :], below], axis=1)
            - 4.0 * rates_f32
        )
        forcing = -decay_row * u + synth_field + lateral * lateral_term + drive_f32
        u = u + time_step * forcing
    return u


def dispatch(activity, drive, basis, *rest):
    npop, nlat, nlon = activity.shape
    owned, half_lat, deg = basis.shape
    fits = (
        lax.axis_size("lon") == 2
        and lax.axis_size("pop") == 2
        and lax.axis_size("band") % 2 == 0
        and npop == 4
        and owned % 16 == 0
        and nlat % 16 == 0
        and (npop * nlat) % LANES == 0
        and nlon % LANES == 0
        and deg % LANES == 0
        and 2 * basis.size <= 40 * 2**20
    )
    return (fast_local if fits else local)(activity, drive, basis, *rest)


def solution(mesh):
    in_specs = (
        P(("subj", "pop"), "band", "lon"),
        P(("subj", "pop"), "band", "lon"),
        P(("subj", "band", "lon"), None, None),
        P(),
        P(),
        P("subj", None),
        P("subj", None),
    )
    out_specs = P(("subj", "pop"), "band", "lon")
    return jax.shard_map(
        dispatch, mesh=mesh, in_specs=in_specs, out_specs=out_specs, check_vma=False
    )
```

```python
import functools
import math

import jax
import jax.numpy as jnp
from jax import lax
from jax.experimental import pallas as pl
from jax.experimental.pallas import tpu as pltpu
from jax.sharding import PartitionSpec as P

NLAT = 640
NLON = 1280
DEG = 640
STEPS = 2


time_step = 0.5


def with_halo(shard, sides, width):
    for axis, dim in sides:
        size, length = (lax.axis_size(axis), shard.shape[dim])
        up = [(i, (i + 1) % size) for i in range(size - 1)]
        down = [(j, i) for i, j in up]
        last = lax.slice_in_dim(shard, length - width, length, axis=dim)
        leading = lax.slice_in_dim(shard, 0, width, axis=dim)
        before = lax.ppermute(last, axis, up)
        after = lax.ppermute(leading, axis, down)
        shard = jnp.concatenate([before, shard, after], axis=dim)
    return shard


def fourier_table():
    longitude = jnp.arange(NLON, dtype=jnp.int32)
    wavenumber = jnp.arange(DEG, dtype=jnp.int32)
    phase = longitude[:, None] * wavenumber[None, :] % NLON
    angle = phase.astype(jnp.float32) * (2.0 * math.pi / NLON)
    return jnp.stack([jnp.cos(angle), jnp.sin(angle)], axis=1).astype(jnp.bfloat16)


def lat_weights():
    row_index = jnp.arange(NLAT // 2, dtype=jnp.float32)
    colatitude = math.pi * (4.0 * row_index + 3.0) / (4.0 * NLAT + 2.0)
    return math.pi * jnp.sin(colatitude) / NLAT


def to_owners(fourier):
    return lax.all_to_all(fourier, ("band", "lon"), split_axis=2, concat_axis=3, tiled=True)


def to_latitudes(synthesis):
    return lax.all_to_all(synthesis, ("band", "lon"), split_axis=3, concat_axis=2, tiled=True)


def local(activity, drive, basis, kernels, conn_block, coupling, rate_params):
    pop_here = activity.shape[0]
    owned_count = basis.shape[0]
    half_lat = basis.shape[1]
    quarter = DEG // 2
    owner_index = lax.axis_index("band") * lax.axis_size("lon") + lax.axis_index("lon")
    pop_first = lax.axis_index("pop") * pop_here
    params = lax.dynamic_slice_in_dim(rate_params, pop_first, pop_here, 1)
    gain_row, thresh, decay_row, lateral = (params[0], params[1], params[2], params[3])
    cos_sin = fourier_table()
    weights = lat_weights()
    wavenumber = owner_index * owned_count + jnp.arange(owned_count, dtype=jnp.int32)
    degree = jnp.arange(DEG, dtype=jnp.int32)
    triangle = degree[None, :] >= wavenumber[:, None]
    slots = jnp.arange(2, dtype=jnp.int32)
    parity_pick = (slots[None, :] == (wavenumber % 2)[:, None])[None, None, :, :, None]
    every_wave = jnp.arange(DEG, dtype=jnp.int32)
    amplitude = jnp.where(every_wave == 0, 1.0, 2.0).astype(jnp.bfloat16)
    coup_own = lax.dynamic_slice_in_dim(coupling, pop_first, pop_here, 0)
    block_own = lax.dynamic_slice_in_dim(conn_block, pop_first, pop_here, 0)
    onehot = (block_own[..., None] == jnp.arange(kernels.shape[0], dtype=jnp.int32)).astype(
        jnp.float32
    )
    mixing = coup_own[..., None] * jnp.einsum(
        "ijb,bn->ijn", onehot, kernels, precision=lax.Precision.HIGHEST
    )
    basis_split = basis.reshape(owned_count, half_lat, quarter, 2)
    drive_f32 = drive.astype(jnp.float32)
    activity_now = activity
    for step_index in range(STEPS):
        rates = jax.nn.sigmoid(
            gain_row[:, None, None] * (activity_now - thresh[:, None, None])
        ).astype(jnp.bfloat16)
        lat_rows = lax.all_to_all(rates, "lon", split_axis=1, concat_axis=2, tiled=True)
        fourier = jnp.einsum(
            "ijk,kcm->icmj", lat_rows, cos_sin, preferred_element_type=jnp.float32
        ).astype(jnp.bfloat16)
        spectrum = to_owners(fourier)
        northern = spectrum[..., :half_lat].astype(jnp.float32)
        southern = jnp.flip(spectrum[..., half_lat:], axis=3).astype(jnp.float32)
        even_part = (weights * (northern + southern)).astype(jnp.bfloat16)
        odd_part = (weights * (northern - southern)).astype(jnp.bfloat16)
        operand = jnp.where(parity_pick, even_part[:, :, :, None, :], odd_part[:, :, :, None, :])
        coeffs = jnp.einsum(
            "icmsj,mjqs->icmqs", operand, basis_split, preferred_element_type=jnp.float32
        )
        coeffs = coeffs.reshape(pop_here, 2, owned_count, DEG)
        coeffs = jnp.where(triangle[None, None], coeffs, 0.0)
        gathered = lax.all_gather(coeffs.astype(jnp.bfloat16), "pop", axis=0, tiled=True).astype(
            coeffs.dtype
        )
        mixed_spec = jnp.sum(mixing[:, :, None, None, :] * gathered[None], axis=1).astype(
            jnp.bfloat16
        )
        degree_parts = jnp.einsum(
            "icmqs,mjqs->icmsj",
            mixed_spec.reshape(pop_here, 2, owned_count, quarter, 2),
            basis_split,
            preferred_element_type=jnp.float32,
        )
        same_parity = jnp.sum(jnp.where(parity_pick, degree_parts, 0.0), axis=3)
        other_parity = jnp.sum(jnp.where(parity_pick, 0.0, degree_parts), axis=3)
        synthesis = jnp.concatenate(
            [same_parity + other_parity, jnp.flip(same_parity - other_parity, axis=3)], axis=3
        ).astype(jnp.bfloat16)
        returned = to_latitudes(synthesis)
        scaled = returned * amplitude[None, None, :, None]
        synth_field = jnp.einsum(
            "icmj,kcm->ijk", scaled, cos_sin, preferred_element_type=jnp.float32
        ) * (1.0 / NLON)
        padded = with_halo(lat_rows, ((("band", "lon"), 1),), 1).astype(jnp.float32)
        rates_f32 = lat_rows.astype(jnp.float32)
        lateral_term = (
            jnp.roll(rates_f32, 1, axis=2)
            + jnp.roll(rates_f32, -1, axis=2)
            + padded[:, 2:, :]
            + padded[:, :-2, :]
            - 4.0 * rates_f32
        )
        coupled = synth_field + lateral[:, None, None] * lateral_term
        coupled_grid = lax.all_to_all(
            coupled.astype(jnp.bfloat16), "lon", split_axis=2, concat_axis=1, tiled=True
        ).astype(coupled.dtype)
        forcing = -decay_row[:, None, None] * activity_now + coupled_grid + drive_f32
        activity_now = activity_now + time_step * forcing
    return activity_now


MESH = pl.DeviceIdType.MESH
LANES = 128


def greet(nband):
    band, lon = lax.axis_index("band"), lax.axis_index("lon")
    barrier = pltpu.get_barrier_semaphore()
    for d in range(1, nband):
        peer = {"band": lax.rem(band + d, nband)}
        pl.semaphore_signal(barrier, inc=1, device_id=peer, device_id_type=MESH)
    pl.semaphore_signal(barrier, inc=1, device_id={"lon": 1 - lon}, device_id_type=MESH)
    pl.semaphore_wait(barrier, nband)


def remote(src, dst, send_sem, recv_sem, peer):
    return pltpu.make_async_remote_copy(
        src_ref=src, dst_ref=dst, send_sem=send_sem, recv_sem=recv_sem,
        device_id=peer, device_id_type=MESH,
    )


def forward_kernel(nband, r_ref, t_ref, e_ref, g_ref, rp_ref, eo_ref, f_ref, xs, xr, zs, zr, es, er):
    band, lon = lax.axis_index("band"), lax.axis_index("lon")
    rows, nlon = r_ref.shape
    block = t_ref.shape[0] // nband
    chunks = rows // LANES
    greet(nband)
    copies = []
    arrivals = []
    for q in range(chunks):
        part = pl.ds(q * LANES, LANES)
        copy = remote(r_ref.at[part], rp_ref.at[part], xs.at[q], xr.at[q], {"lon": 1 - lon})
        copy.start()
        arrivals.append(copy)
    for side, step in ((0, 1), (1, nband - 1)):
        peer = {"band": lax.rem(band + step, nband)}
        copy = remote(e_ref.at[side], eo_ref.at[side], es.at[side], er.at[side], peer)
        copy.start()
        copies.append(copy)
    contract = (((1,), (1,)), ((), ()))
    for q in range(chunks):
        part = pl.ds(q * LANES, LANES)
        total = lax.dot_general(
            t_ref[:, :nlon], r_ref[part, :], contract, preferred_element_type=jnp.float32
        )
        arrivals[q].wait_recv()
        total += lax.dot_general(
            t_ref[:, nlon:], rp_ref[part, :], contract, preferred_element_type=jnp.float32
        )
        f_ref[q] = total.astype(f_ref.dtype)
        for d in range(1, nband):
            dest = lax.rem(band + d, nband)
            rows_out = pl.ds(pl.multiple_of(dest * block, 16), block)
            copy = remote(
                f_ref.at[q, rows_out], g_ref.at[band, :, part],
                zs.at[q, d - 1], zr.at[q, d - 1], {"band": dest},
            )
            copy.start()
            copies.append(copy)
        own = pl.ds(pl.multiple_of(band * block, 16), block)
        g_ref[band, :, part] = f_ref[q, own]
    for copy in arrivals:
        copy.wait_send()
    for copy in copies:
        copy.wait()


def forward(rates, table, edges, nband):
    rows, nlon = rates.shape
    width = table.shape[0]
    chunks = rows // LANES
    dma = pltpu.SemaphoreType.DMA
    vmem = pl.BlockSpec(memory_space=pltpu.VMEM)
    return pl.pallas_call(
        functools.partial(forward_kernel, nband),
        out_shape=(
            jax.ShapeDtypeStruct((nband, width // nband, rows), jnp.bfloat16),
            jax.ShapeDtypeStruct((rows, nlon), jnp.bfloat16),
            jax.ShapeDtypeStruct(edges.shape, jnp.bfloat16),
        ),
        in_specs=[vmem] * 3,
        out_specs=(vmem,) * 3,
        scratch_shapes=[
            pltpu.VMEM((chunks, width, LANES), jnp.bfloat16),
            dma((chunks,)), dma((chunks,)),
            dma((chunks, nband - 1)), dma((chunks, nband - 1)),
            dma((2,)), dma((2,)),
        ],
        compiler_params=pltpu.CompilerParams(collective_id=0, has_side_effects=True),
        name="forward_exchange",
    )(rates, table, edges)


def backward_kernel(nband, last, s_ref, t_ref, mir_ref, flip_ref, rates_ref, rp_ref, eo_ref, u_ref, drive_ref,
                    par_ref, *rest):
    if last:
        un_ref, m_ref, o_ref, field_ref, pad_ref, zs, zr, xs, xr = rest
    else:
        un_ref, rn_ref, fn_ref, en_ref, m_ref, o_ref, field_ref, pad_ref, zs, zr, xs, xr = rest
    band, lon = lax.axis_index("band"), lax.axis_index("lon")
    _, block, rows = s_ref.shape
    npop, nlat, nlon = rates_ref.shape
    hb = nband // 2
    half = nband * block
    chunks = rows // LANES
    partner = {"lon": 1 - lon}
    greet(nband)
    for h in range(hb):
        m_ref[h] = s_ref[h]
        m_ref[hb + h] = jnp.dot(
            s_ref[hb + h], mir_ref[...], preferred_element_type=jnp.float32
        ).astype(m_ref.dtype)
    crossing = []
    along = []
    for q in range(chunks):
        part = pl.ds(q * LANES, LANES)
        for d in range(1, nband):
            dest = lax.rem(band + d, nband)
            copy = remote(
                m_ref.at[dest, :, part], o_ref.at[0, band, :, part],
                zs.at[q, d - 1], zr.at[q, d - 1], {"band": dest},
            )
            copy.start()
            along.append(copy)
    for q in range(chunks):
        part = pl.ds(q * LANES, LANES)
        copy = remote(
            m_ref.at[band, :, part], o_ref.at[1, band, :, part], xs.at[q, 0], xr.at[q, 0], partner
        )
        copy.start()
        crossing.append([copy])
    o_ref[0, band] = m_ref[band]
    contract = (((0,), (0,)), ((), ()))
    for q in range(chunks):
        part = pl.ds(q * LANES, LANES)
        for d in range(1, nband):
            along[q * (nband - 1) + d - 1].wait_recv()
            source = lax.rem(band + nband - d, nband)
            copy = remote(
                o_ref.at[0, source, :, part], o_ref.at[1, source, :, part],
                xs.at[q, d], xr.at[q, d], partner,
            )
            copy.start()
            crossing[q].append(copy)
        field_ref[part] = lax.dot_general(
            o_ref[0, :, :, part].reshape(half, LANES), t_ref[:half], contract,
            preferred_element_type=jnp.float32,
        )
    for q in range(chunks):
        part = pl.ds(q * LANES, LANES)
        for copy in crossing[q]:
            copy.wait_recv()
        field_ref[part] += lax.dot_general(
            o_ref[1, :, :, part].reshape(half, LANES), t_ref[half:], contract,
            preferred_element_type=jnp.float32,
        )
    step = 16
    scale = 1.0 / (2 * nlon)
    column = lax.broadcasted_iota(jnp.int32, (step, nlon), 1)

    @pl.loop(0, npop)
    def _(i):
        gain, thresh, decay, lateral = (par_ref[k, i] for k in range(4))
        base = pl.multiple_of(i * nlat, step)
        pad_ref[pl.ds(8, nlat)] = rates_ref[i].astype(jnp.float32)
        around = eo_ref[:, i].astype(jnp.float32)
        pad_ref[7:8] = jnp.where(band > 0, around[0, 0:1], 0.0)
        pad_ref[8 + nlat : 9 + nlat] = jnp.where(band < nband - 1, around[1, 0:1], 0.0)
        facing = rp_ref[pl.ds(base, nlat)]
        west = jnp.dot(flip_ref[...], facing[:, nlon - LANES :], preferred_element_type=jnp.float32)
        east = jnp.dot(flip_ref[...], facing[:, :LANES], preferred_element_type=jnp.float32)
        for r in range(0, nlat, step):
            here = pl.ds(base + r, step)
            own = pad_ref[8 + r : 8 + r + step]
            beside = (
                jnp.where(column == 0, west[r : r + step, LANES - 1 :], pltpu.roll(own, 1, 1))
                + jnp.where(column == nlon - 1, east[r : r + step, :1], pltpu.roll(own, nlon - 1, 1))
                + pad_ref[9 + r : 9 + r + step]
                + pad_ref[7 + r : 7 + r + step]
                - 4.0 * own
            )
            u = u_ref[here]
            forcing = (
                -decay * u + field_ref[here] * scale + lateral * beside
                + drive_ref[here].astype(jnp.float32)
            )
            u = u + time_step * forcing
            un_ref[here] = u
            if not last:
                rn_ref[i, r : r + step] = jax.nn.sigmoid(gain * (u - thresh)).astype(rn_ref.dtype)
        if not last:
            fresh = rn_ref[i]
            fn_ref[pl.ds(base, nlat)] = jnp.dot(
                flip_ref[...], fresh, preferred_element_type=jnp.float32
            ).astype(fn_ref.dtype)
            en_ref[0, i] = jnp.broadcast_to(fresh[nlat - 1 :], en_ref.shape[2:])
            en_ref[1, i] = jnp.broadcast_to(fresh[:1], en_ref.shape[2:])

    for copy in along:
        copy.wait_send()
    for group in crossing:
        for copy in group:
            copy.wait_send()


def backward(synthesis, table, mirrors, flip, rates, partner, around, u, drive, params, nband, last):
    rows = synthesis.shape[2]
    npop, nlat, nlon = rates.shape
    chunks = rows // LANES
    dma = pltpu.SemaphoreType.DMA
    vmem = pl.BlockSpec(memory_space=pltpu.VMEM)
    shapes = [jax.ShapeDtypeStruct(u.shape, jnp.float32)]
    if not last:
        shapes += [
            jax.ShapeDtypeStruct(rates.shape, jnp.bfloat16),
            jax.ShapeDtypeStruct(partner.shape, jnp.bfloat16),
            jax.ShapeDtypeStruct(around.shape, jnp.bfloat16),
        ]
    return pl.pallas_call(
        functools.partial(backward_kernel, nband, last),
        out_shape=tuple(shapes),
        in_specs=[vmem] * 9 + [pl.BlockSpec(memory_space=pltpu.SMEM)],
        out_specs=(vmem,) * len(shapes),
        scratch_shapes=[
            pltpu.VMEM(synthesis.shape, jnp.bfloat16),
            pltpu.VMEM((2,) + synthesis.shape, jnp.bfloat16),
            pltpu.VMEM((rows, nlon), jnp.float32),
            pltpu.VMEM((nlat + 16, nlon), jnp.float32),
            dma((chunks, nband - 1)), dma((chunks, nband - 1)),
            dma((chunks, nband)), dma((chunks, nband)),
        ],
        compiler_params=pltpu.CompilerParams(
            collective_id=3 if last else 1, has_side_effects=True, vmem_limit_bytes=40 * 2**20
        ),
        name="backward_last" if last else "backward_exchange",
    )(synthesis, table, mirrors, flip, rates, partner, around, u, drive, params)


def spectral_kernel(group, nband, g_ref, w_ref, b_hbm, a_ref, k_ref, s_ref, b_ref, own_ref, other_ref,
                    x_ref, y_ref, bsem, ss, rs):
    owned, half_lat, deg = b_ref.shape
    half = own_ref.shape[1]
    both = 2 * half
    npop = half // 2
    hb = nband // 2
    nlat = half_lat // hb
    owner = lax.axis_index("band") * lax.axis_size("lon") + lax.axis_index("lon")
    first = owner * owned
    chunks = owned // group
    kinds = k_ref.shape[0]
    partner = {"pop": 1 - lax.axis_index("pop")}

    def fetch(c):
        part = pl.ds(c * group, group)
        return pltpu.make_async_copy(b_hbm.at[part], b_ref.at[part], bsem.at[c])

    def swap(c):
        part = pl.ds(c * group, group)
        return remote(own_ref.at[part], other_ref.at[part], ss.at[c], rs.at[c], partner)

    def lines(cc, c):
        return pl.ds(pl.multiple_of(cc * owned + c * group, group), group)

    @pl.loop(0, chunks)
    def _(c):
        fetch(c).start()

    barrier = pltpu.get_barrier_semaphore()
    pl.semaphore_signal(barrier, inc=1, device_id=partner, device_id_type=MESH)
    pl.semaphore_wait(barrier, 1)
    degree = lax.broadcasted_iota(jnp.int32, (half, deg), 1)
    tiles = x_ref.shape[0]
    spare = tiles * LANES - half_lat
    padding = [jnp.zeros((group, spare), jnp.float32)] if spare else []
    wide_padding = [jnp.zeros((both, spare), jnp.float32)] if spare else []

    @pl.loop(0, chunks)
    def _(c):
        for cc in range(2):
            parts = []
            for h in range(hb):
                north = g_ref[h, lines(cc, c), :].astype(jnp.float32)
                south = g_ref[nband - 1 - h, lines(cc, c), :].astype(jnp.float32)
                parts.append((w_ref[h] * (north + south), w_ref[h] * (north - south)))
            for side in range(2):
                for i in range(npop):
                    row = side * half + i * 2 + cc
                    line = [part[side][:, i * nlat : (i + 1) * nlat] for part in parts]
                    line = jnp.concatenate(line + padding, axis=1)
                    for t in range(tiles):
                        x_ref[t, pl.ds(row, group, stride=both), :] = line[
                            :, t * LANES : (t + 1) * LANES
                        ]
        fetch(c).wait()
        for g in range(group):
            m = c * group + g
            x = [x_ref[t, g * both : (g + 1) * both, :] for t in range(tiles)]
            x = jnp.concatenate(x, axis=1)[:, :half_lat].astype(jnp.bfloat16)
            parity = jnp.dot(x, b_ref[m], preferred_element_type=jnp.float32)
            gap = degree - (first + m)
            coeffs = jnp.where(gap % 2 == 0, parity[:half], parity[half:])
            own_ref[m] = jnp.where(gap >= 0, coeffs, 0.0).astype(own_ref.dtype)
        swap(c).start()

    @pl.loop(0, chunks)
    def _(c):
        swap(c).wait_recv()
        for g in range(group):
            m = c * group + g
            pair = jnp.concatenate(
                [own_ref[m].astype(jnp.float32), other_ref[m].astype(jnp.float32)], axis=0
            ).astype(jnp.bfloat16)
            by_kind = jnp.dot(
                a_ref[...], jnp.concatenate([pair, pair], axis=0),
                preferred_element_type=jnp.float32,
            )
            mixed = k_ref[0:1] * by_kind[:half]
            for kind in range(1, kinds):
                mixed += k_ref[kind : kind + 1] * by_kind[kind * half : (kind + 1) * half]
            gap = degree - (first + m)
            signed = jnp.where(gap % 2 == 0, mixed, -mixed)
            y = lax.dot_general(
                jnp.concatenate([mixed, signed], axis=0).astype(jnp.bfloat16), b_ref[m],
                (((1,), (1,)), ((), ())), preferred_element_type=jnp.float32,
            )
            y = jnp.concatenate([y] + wide_padding, axis=1)
            for t in range(tiles):
                y_ref[t, g * both : (g + 1) * both, :] = y[:, t * LANES : (t + 1) * LANES]
        for side in range(2):
            for cc in range(2):
                rows = [
                    jnp.concatenate(
                        [
                            y_ref[t, pl.ds(side * half + i * 2 + cc, group, stride=both), :]
                            for t in range(tiles)
                        ],
                        axis=1,
                    )
                    for i in range(npop)
                ]
                for h in range(hb):
                    dest = h if side == 0 else nband - 1 - h
                    s_ref[dest, lines(cc, c), :] = jnp.concatenate(
                        [row[:, h * nlat : (h + 1) * nlat] for row in rows], axis=1
                    ).astype(s_ref.dtype)

    @pl.loop(0, chunks)
    def _(c):
        swap(c).wait_send()


def spectral(spectrum, weights, basis, by_kind, kernels, npop):
    owned, half_lat, deg = basis.shape
    nband = spectrum.shape[0]
    group = 16
    chunks = owned // group
    dma = pltpu.SemaphoreType.DMA
    vmem = pl.BlockSpec(memory_space=pltpu.VMEM)
    return pl.pallas_call(
        functools.partial(spectral_kernel, group, nband),
        out_shape=jax.ShapeDtypeStruct(spectrum.shape, jnp.bfloat16),
        in_specs=[vmem, vmem, pl.BlockSpec(memory_space=pltpu.MemorySpace.HBM), vmem, vmem],
        out_specs=vmem,
        scratch_shapes=[
            pltpu.VMEM(basis.shape, jnp.bfloat16),
            pltpu.VMEM((owned, 2 * npop, deg), jnp.bfloat16),
            pltpu.VMEM((owned, 2 * npop, deg), jnp.bfloat16),
            pltpu.VMEM((pl.cdiv(half_lat, LANES), group * 4 * npop, LANES), jnp.float32),
            pltpu.VMEM((pl.cdiv(half_lat, LANES), group * 4 * npop, LANES), jnp.float32),
            dma((chunks,)), dma((chunks,)), dma((chunks,)),
        ],
        compiler_params=pltpu.CompilerParams(
            collective_id=2, has_side_effects=True, vmem_limit_bytes=56 * 2**20
        ),
        name="spectral_mix",
    )(spectrum, weights, basis, by_kind, kernels)


def wave_table(starts, owned, longitude, period):
    coarse = starts[:, None] + 16 * jnp.arange(owned // 16, dtype=jnp.int32)[None, :]
    fine = jnp.arange(16, dtype=jnp.int32)

    def angles(wave):
        phase = wave[..., None] * longitude % period
        angle = phase.astype(jnp.float32) * (2.0 * math.pi / period)
        return lax.optimization_barrier((jnp.cos(angle), jnp.sin(angle)))

    cos_a, sin_a = (v[:, :, None, :] for v in angles(coarse))
    cos_b, sin_b = (v[None, None, :, :] for v in angles(fine))
    shape = (starts.shape[0], owned, longitude.shape[0])
    cosine = (cos_a * cos_b - sin_a * sin_b).reshape(shape)
    sine = (sin_a * cos_b + cos_a * sin_b).reshape(shape)
    return jnp.stack([cosine, sine], axis=1)


def fast_local(activity, drive, basis, kernels, conn_block, coupling, rate_params):
    npop, nlat, nlon = activity.shape
    owned, half_lat, deg = basis.shape
    nband = lax.axis_size("band")
    hb = nband // 2
    period = nlon * lax.axis_size("lon")
    rows = npop * nlat
    band, lon, pop = lax.axis_index("band"), lax.axis_index("lon"), lax.axis_index("pop")
    pop_first = pop * npop
    params = lax.dynamic_slice_in_dim(rate_params, pop_first, npop, 1)
    gain_row, thresh = params[0, :, None, None], params[1, :, None, None]

    bands = jnp.arange(nband, dtype=jnp.int32)
    kk = jnp.arange(nlon, dtype=jnp.int32)
    own_start = (bands * 2 + lon) * owned
    other_start = (bands * 2 + 1 - lon) * owned
    k_order = jnp.concatenate([lon * nlon + kk, (1 - lon) * nlon + kk])
    analysis_table = (
        wave_table(own_start, owned, k_order, period).reshape(deg, period).astype(jnp.bfloat16)
    )
    starts = jnp.concatenate([own_start, other_start])
    waves = starts[:, None] + jnp.arange(owned, dtype=jnp.int32)[None, :]
    amplitude = jnp.where(waves == 0, 1.0, 2.0)[:, None, :, None]
    synthesis_table = (
        (wave_table(starts, owned, lon * nlon + kk, period) * amplitude)
        .reshape(2 * deg, nlon)
        .astype(jnp.bfloat16)
    )

    row_index = jnp.arange(half_lat, dtype=jnp.float32)
    colatitude = math.pi * (4.0 * row_index + 3.0) / (8.0 * half_lat + 2.0)
    weights = math.pi * jnp.sin(colatitude) / (2.0 * half_lat)
    weights = jnp.tile(weights.reshape(hb, 1, nlat), (1, 1, npop))

    south = band >= hb
    lat = jnp.arange(nlat, dtype=jnp.int32)
    mirror = (lat[:, None] == jnp.where(south, nlat - 1 - lat, lat)[None, :]).astype(jnp.bfloat16)
    back = (lat[:, None] == nlat - 1 - lat[None, :]).astype(jnp.bfloat16)
    mirrors = jnp.einsum("xy,ab->xayb", jnp.eye(npop, dtype=jnp.bfloat16), back)
    mirrors = mirrors.reshape(rows, rows)

    coup_own = lax.dynamic_slice_in_dim(coupling, pop_first, npop, 0)
    block_own = lax.dynamic_slice_in_dim(conn_block, pop_first, npop, 0)
    kind = jnp.arange(kernels.shape[0], dtype=jnp.int32)
    per_kind = jnp.where(block_own[None] == kind[:, None, None], coup_own[None], 0.0)
    per_kind = jnp.concatenate(
        [
            lax.dynamic_slice_in_dim(per_kind, pop_first, npop, 2),
            lax.dynamic_slice_in_dim(per_kind, (1 - pop) * npop, npop, 2),
        ],
        axis=2,
    )
    spread = per_kind[:, :, None, :, None] * jnp.eye(2, dtype=jnp.float32)[:, None, :]
    spread = spread.reshape(kernels.shape[0] * npop * 2, 2 * npop * 2)
    coarse = lax.reduce_precision(spread, 8, 7)
    by_kind = jnp.concatenate([coarse, spread - coarse], axis=1).astype(jnp.bfloat16)

    drive = drive.reshape(rows, nlon)
    u = activity.reshape(rows, nlon)
    rates = jax.nn.sigmoid(gain_row * (activity - thresh)).astype(jnp.bfloat16)
    facing = jnp.einsum("aj,ijk->iak", mirror, rates, preferred_element_type=jnp.float32)
    facing = facing.astype(jnp.bfloat16).reshape(rows, nlon)
    edges = jnp.stack([rates[:, nlat - 1 :, :], rates[:, :1, :]])
    edges = jnp.broadcast_to(edges, (2, npop, 16, nlon))
    for step_index in range(STEPS):
        spectrum, partner, around = forward(facing, analysis_table, edges, nband)
        outgoing = spectral(spectrum, weights, basis, by_kind, kernels, npop)
        results = backward(
            outgoing, synthesis_table, mirrors, mirror, rates, partner, around, u, drive, params,
            nband, step_index == STEPS - 1,
        )
        if step_index < STEPS - 1:
            u, rates, facing, edges = results
        else:
            (u,) = results
    return u.reshape(npop, nlat, nlon)


def dispatch(activity, drive, basis, *rest):
    npop, nlat, nlon = activity.shape
    owned, half_lat, deg = basis.shape
    fits = (
        lax.axis_size("lon") == 2
        and lax.axis_size("pop") == 2
        and lax.axis_size("band") % 2 == 0
        and npop == 4
        and owned % 16 == 0
        and nlat % 16 == 0
        and (npop * nlat) % LANES == 0
        and nlon % LANES == 0
        and deg % LANES == 0
        and 2 * basis.size <= 40 * 2**20
    )
    return (fast_local if fits else local)(activity, drive, basis, *rest)


def solution(mesh):
    in_specs = (
        P(("subj", "pop"), "band", "lon"),
        P(("subj", "pop"), "band", "lon"),
        P(("subj", "band", "lon"), None, None),
        P(),
        P(),
        P("subj", None),
        P("subj", None),
    )
    out_specs = P(("subj", "pop"), "band", "lon")
    return jax.shard_map(
        dispatch, mesh=mesh, in_specs=in_specs, out_specs=out_specs, check_vma=False
    )
```

```python
import functools
import math

import jax
import jax.numpy as jnp
from jax import lax
from jax.experimental import pallas as pl
from jax.experimental.pallas import tpu as pltpu
from jax.sharding import PartitionSpec as P

NLAT = 640
NLON = 1280
DEG = 640
STEPS = 2


time_step = 0.5


def with_halo(shard, sides, width):
    for axis, dim in sides:
        size, length = (lax.axis_size(axis), shard.shape[dim])
        up = [(i, (i + 1) % size) for i in range(size - 1)]
        down = [(j, i) for i, j in up]
        last = lax.slice_in_dim(shard, length - width, length, axis=dim)
        leading = lax.slice_in_dim(shard, 0, width, axis=dim)
        before = lax.ppermute(last, axis, up)
        after = lax.ppermute(leading, axis, down)
        shard = jnp.concatenate([before, shard, after], axis=dim)
    return shard


def fourier_table():
    longitude = jnp.arange(NLON, dtype=jnp.int32)
    wavenumber = jnp.arange(DEG, dtype=jnp.int32)
    phase = longitude[:, None] * wavenumber[None, :] % NLON
    angle = phase.astype(jnp.float32) * (2.0 * math.pi / NLON)
    return jnp.stack([jnp.cos(angle), jnp.sin(angle)], axis=1).astype(jnp.bfloat16)


def lat_weights():
    row_index = jnp.arange(NLAT // 2, dtype=jnp.float32)
    colatitude = math.pi * (4.0 * row_index + 3.0) / (4.0 * NLAT + 2.0)
    return math.pi * jnp.sin(colatitude) / NLAT


def to_owners(fourier):
    return lax.all_to_all(fourier, ("band", "lon"), split_axis=2, concat_axis=3, tiled=True)


def to_latitudes(synthesis):
    return lax.all_to_all(synthesis, ("band", "lon"), split_axis=3, concat_axis=2, tiled=True)


def local(activity, drive, basis, kernels, conn_block, coupling, rate_params):
    pop_here = activity.shape[0]
    owned_count = basis.shape[0]
    half_lat = basis.shape[1]
    quarter = DEG // 2
    owner_index = lax.axis_index("band") * lax.axis_size("lon") + lax.axis_index("lon")
    pop_first = lax.axis_index("pop") * pop_here
    params = lax.dynamic_slice_in_dim(rate_params, pop_first, pop_here, 1)
    gain_row, thresh, decay_row, lateral = (params[0], params[1], params[2], params[3])
    cos_sin = fourier_table()
    weights = lat_weights()
    wavenumber = owner_index * owned_count + jnp.arange(owned_count, dtype=jnp.int32)
    degree = jnp.arange(DEG, dtype=jnp.int32)
    triangle = degree[None, :] >= wavenumber[:, None]
    slots = jnp.arange(2, dtype=jnp.int32)
    parity_pick = (slots[None, :] == (wavenumber % 2)[:, None])[None, None, :, :, None]
    every_wave = jnp.arange(DEG, dtype=jnp.int32)
    amplitude = jnp.where(every_wave == 0, 1.0, 2.0).astype(jnp.bfloat16)
    coup_own = lax.dynamic_slice_in_dim(coupling, pop_first, pop_here, 0)
    block_own = lax.dynamic_slice_in_dim(conn_block, pop_first, pop_here, 0)
    onehot = (block_own[..., None] == jnp.arange(kernels.shape[0], dtype=jnp.int32)).astype(
        jnp.float32
    )
    mixing = coup_own[..., None] * jnp.einsum(
        "ijb,bn->ijn", onehot, kernels, precision=lax.Precision.HIGHEST
    )
    basis_split = basis.reshape(owned_count, half_lat, quarter, 2)
    drive_f32 = drive.astype(jnp.float32)
    activity_now = activity
    for step_index in range(STEPS):
        rates = jax.nn.sigmoid(
            gain_row[:, None, None] * (activity_now - thresh[:, None, None])
        ).astype(jnp.bfloat16)
        lat_rows = lax.all_to_all(rates, "lon", split_axis=1, concat_axis=2, tiled=True)
        fourier = jnp.einsum(
            "ijk,kcm->icmj", lat_rows, cos_sin, preferred_element_type=jnp.float32
        ).astype(jnp.bfloat16)
        spectrum = to_owners(fourier)
        northern = spectrum[..., :half_lat].astype(jnp.float32)
        southern = jnp.flip(spectrum[..., half_lat:], axis=3).astype(jnp.float32)
        even_part = (weights * (northern + southern)).astype(jnp.bfloat16)
        odd_part = (weights * (northern - southern)).astype(jnp.bfloat16)
        operand = jnp.where(parity_pick, even_part[:, :, :, None, :], odd_part[:, :, :, None, :])
        coeffs = jnp.einsum(
            "icmsj,mjqs->icmqs", operand, basis_split, preferred_element_type=jnp.float32
        )
        coeffs = coeffs.reshape(pop_here, 2, owned_count, DEG)
        coeffs = jnp.where(triangle[None, None], coeffs, 0.0)
        gathered = lax.all_gather(coeffs.astype(jnp.bfloat16), "pop", axis=0, tiled=True).astype(
            coeffs.dtype
        )
        mixed_spec = jnp.sum(mixing[:, :, None, None, :] * gathered[None], axis=1).astype(
            jnp.bfloat16
        )
        degree_parts = jnp.einsum(
            "icmqs,mjqs->icmsj",
            mixed_spec.reshape(pop_here, 2, owned_count, quarter, 2),
            basis_split,
            preferred_element_type=jnp.float32,
        )
        same_parity = jnp.sum(jnp.where(parity_pick, degree_parts, 0.0), axis=3)
        other_parity = jnp.sum(jnp.where(parity_pick, 0.0, degree_parts), axis=3)
        synthesis = jnp.concatenate(
            [same_parity + other_parity, jnp.flip(same_parity - other_parity, axis=3)], axis=3
        ).astype(jnp.bfloat16)
        returned = to_latitudes(synthesis)
        scaled = returned * amplitude[None, None, :, None]
        synth_field = jnp.einsum(
            "icmj,kcm->ijk", scaled, cos_sin, preferred_element_type=jnp.float32
        ) * (1.0 / NLON)
        padded = with_halo(lat_rows, ((("band", "lon"), 1),), 1).astype(jnp.float32)
        rates_f32 = lat_rows.astype(jnp.float32)
        lateral_term = (
            jnp.roll(rates_f32, 1, axis=2)
            + jnp.roll(rates_f32, -1, axis=2)
            + padded[:, 2:, :]
            + padded[:, :-2, :]
            - 4.0 * rates_f32
        )
        coupled = synth_field + lateral[:, None, None] * lateral_term
        coupled_grid = lax.all_to_all(
            coupled.astype(jnp.bfloat16), "lon", split_axis=2, concat_axis=1, tiled=True
        ).astype(coupled.dtype)
        forcing = -decay_row[:, None, None] * activity_now + coupled_grid + drive_f32
        activity_now = activity_now + time_step * forcing
    return activity_now


MESH = pl.DeviceIdType.MESH
LANES = 128


def remote(src, dst, send_sem, recv_sem, peer):
    return pltpu.make_async_remote_copy(
        src_ref=src, dst_ref=dst, send_sem=send_sem, recv_sem=recv_sem,
        device_id=peer, device_id_type=MESH,
    )


def step_kernel(nband, last, rates_ref, t_ref, mirror_ref, mirrors_ref, w_ref, b_hbm, a_ref, k_ref,
                u_ref, drive_ref, par_ref, *rest):
    if last:
        un_ref, *rest = rest
    else:
        un_ref, rn_ref, *rest = rest
    (face_ref, ps_ref, pr_ref, fz_ref, gz_ref, b_ref, own_ref, other_ref, x_ref, y_ref, s_ref, o_ref,
     field_ref, pad_ref, edge_ref, around_ref, af_ref, col_ref, side_ref, we_ref,
     bsem, ps, pr, zs, zr, ss, rs, ys, yr, xs, xr, es, er) = rest
    band, lon = lax.axis_index("band"), lax.axis_index("lon")
    rows, nlon = rates_ref.shape
    owned, half_lat, deg = b_ref.shape
    groups = t_ref.shape[0]
    group = owned // groups
    half = own_ref.shape[1]
    both = 2 * half
    npop = half // 2
    hb = nband // 2
    nlat = half_lat // hb
    lines = 2 * group
    first = (band * lax.axis_size("lon") + lon) * owned
    kinds = k_ref.shape[0]
    across = {"lon": 1 - lon}
    mate = {"pop": 1 - lax.axis_index("pop")}
    tiles = x_ref.shape[0]
    spare = tiles * LANES - half_lat
    padding = [jnp.zeros((group, spare), jnp.float32)] if spare else []
    wide_padding = [jnp.zeros((both, spare), jnp.float32)] if spare else []
    degree = lax.broadcasted_iota(jnp.int32, (half, deg), 1)
    along = (((1,), (1,)), ((), ()))
    down = (((0,), (0,)), ((), ()))

    def forward_band(d):
        return lax.rem(band + d, nband)

    def backward_band(d):
        return lax.rem(band + nband - d, nband)

    def fetch(g):
        part = pl.ds(g * group, group)
        return pltpu.make_async_copy(b_hbm.at[part], b_ref.at[part], bsem.at[g])

    def partial(g):
        return remote(ps_ref.at[g], pr_ref.at[g], ps.at[g], pr.at[g], across)

    def outward(g, d):
        dest = forward_band(d)
        return remote(
            fz_ref.at[g, dest], gz_ref.at[g, band], zs.at[g, d - 1], zr.at[g, d - 1], {"band": dest}
        )

    def swap(g):
        part = pl.ds(g * group, group)
        return remote(own_ref.at[part], other_ref.at[part], ss.at[g], rs.at[g], mate)

    def homeward(g, d):
        dest = forward_band(d)
        return remote(
            s_ref.at[g, dest], o_ref.at[g, 0, band], ys.at[g, d - 1], yr.at[g, d - 1], {"band": dest}
        )

    def cross(g, d):
        source = backward_band(d)
        block = s_ref.at[g, band] if d == 0 else o_ref.at[g, 0, source]
        return remote(block, o_ref.at[g, 1, source], xs.at[g, d], xr.at[g, d], across)

    def edge(side):
        peer = {"band": forward_band(1 if side == 0 else nband - 1)}
        return remote(edge_ref.at[side], around_ref.at[side], es.at[side], er.at[side], peer)

    def column():
        return remote(col_ref, side_ref, es.at[2], er.at[2], across)

    @pl.loop(0, groups)
    def _(g):
        fetch(g).start()

    barrier = pltpu.get_barrier_semaphore()
    for d in range(1, nband):
        peer = {"band": forward_band(d)}
        pl.semaphore_signal(barrier, inc=1, device_id=peer, device_id_type=MESH)
    pl.semaphore_signal(barrier, inc=1, device_id=across, device_id_type=MESH)
    pl.semaphore_signal(barrier, inc=1, device_id=mate, device_id_type=MESH)

    for i in range(npop):
        part = pl.ds(i * nlat, nlat)
        face_ref[part] = jnp.dot(
            mirror_ref[...], rates_ref[part], preferred_element_type=jnp.float32
        ).astype(face_ref.dtype)
    fill = jnp.zeros((16 - npop, nlon), jnp.float32)
    for side, at in ((0, nlat - 1), (1, 0)):
        picked = [
            rates_ref[i * nlat + at : i * nlat + at + 1].astype(jnp.float32) for i in range(npop)
        ]
        edge_ref[side] = jnp.concatenate(picked + [fill], axis=0).astype(edge_ref.dtype)
    r16 = lax.broadcasted_iota(jnp.int32, (16, nlon), 0)
    c16 = lax.broadcasted_iota(jnp.int32, (16, nlon), 1)
    pick = ((r16 == 0) & (c16 == nlon - 1)) | ((r16 == 1) & (c16 == 0))
    col_ref[...] = lax.dot_general(
        jnp.where(pick, 1.0, 0.0).astype(jnp.bfloat16), rates_ref[...], along,
        preferred_element_type=jnp.float32,
    ).astype(col_ref.dtype)
    pl.semaphore_wait(barrier, nband + 1)

    @pl.loop(0, groups)
    def _(g):
        ps_ref[g] = lax.dot_general(
            t_ref[g, 1], face_ref[...], along, preferred_element_type=jnp.float32
        ).astype(ps_ref.dtype)
        partial(g).start()

    edge(0).start()
    edge(1).start()
    column().start()
    field_ref[...] = jnp.zeros_like(field_ref)

    def analyse_longitudes(g):
        total = lax.dot_general(
            t_ref[g, 0], face_ref[...], along, preferred_element_type=jnp.float32
        )
        partial(g).wait_recv()
        total = (total + pr_ref[g].astype(jnp.float32)).astype(fz_ref.dtype)
        fz_ref[g] = total.reshape(fz_ref.shape[1:])
        for d in range(1, nband):
            outward(g, d).start()
        gz_ref[g, band] = fz_ref[g, band]

    def analyse_latitudes(g):
        for d in range(1, nband):
            outward(g, d).wait_recv()
        for cc in range(2):
            part = slice(cc * group, (cc + 1) * group)
            parts = []
            for h in range(hb):
                north = gz_ref[g, h, part, :].astype(jnp.float32)
                south = gz_ref[g, nband - 1 - h, part, :].astype(jnp.float32)
                parts.append((w_ref[h] * (north + south), w_ref[h] * (north - south)))
            for side in range(2):
                for i in range(npop):
                    row = side * half + i * 2 + cc
                    line = [piece[side][:, i * nlat : (i + 1) * nlat] for piece in parts]
                    line = jnp.concatenate(line + padding, axis=1)
                    for t in range(tiles):
                        x_ref[t, pl.ds(row, group, stride=both), :] = line[
                            :, t * LANES : (t + 1) * LANES
                        ]
        fetch(g).wait()
        for k in range(group):
            m = g * group + k
            x = [x_ref[t, k * both : (k + 1) * both, :] for t in range(tiles)]
            x = jnp.concatenate(x, axis=1)[:, :half_lat].astype(jnp.bfloat16)
            parity = jnp.dot(x, b_ref[m], preferred_element_type=jnp.float32)
            gap = degree - (first + m)
            coeffs = jnp.where(gap % 2 == 0, parity[:half], parity[half:])
            own_ref[m] = jnp.where(gap >= 0, coeffs, 0.0).astype(own_ref.dtype)
        swap(g).start()

    def synthesise(g):
        swap(g).wait_recv()
        for k in range(group):
            m = g * group + k
            pair = jnp.concatenate(
                [own_ref[m].astype(jnp.float32), other_ref[m].astype(jnp.float32)], axis=0
            ).astype(jnp.bfloat16)
            by_kind = jnp.dot(
                a_ref[...], jnp.concatenate([pair, pair], axis=0),
                preferred_element_type=jnp.float32,
            )
            mixed = k_ref[0:1] * by_kind[:half]
            for kind in range(1, kinds):
                mixed += k_ref[kind : kind + 1] * by_kind[kind * half : (kind + 1) * half]
            gap = degree - (first + m)
            signed = jnp.where(gap % 2 == 0, mixed, -mixed)
            y = lax.dot_general(
                jnp.concatenate([mixed, signed], axis=0).astype(jnp.bfloat16), b_ref[m],
                along, preferred_element_type=jnp.float32,
            )
            y = y * jnp.where(first + m == 0, 1.0, 2.0)
            y = jnp.concatenate([y] + wide_padding, axis=1)
            for t in range(tiles):
                y_ref[t, k * both : (k + 1) * both, :] = y[:, t * LANES : (t + 1) * LANES]
        for side in range(2):
            blocks = [[None, None] for h in range(hb)]
            for cc in range(2):
                wide = [
                    jnp.concatenate(
                        [
                            y_ref[t, pl.ds(side * half + i * 2 + cc, group, stride=both), :]
                            for t in range(tiles)
                        ],
                        axis=1,
                    )
                    for i in range(npop)
                ]
                for h in range(hb):
                    blocks[h][cc] = jnp.concatenate(
                        [row[:, h * nlat : (h + 1) * nlat] for row in wide], axis=1
                    ).astype(s_ref.dtype)
            joined = jnp.concatenate([piece for block in blocks for piece in block], axis=0)
            if side == 1:
                joined = jnp.dot(
                    joined, mirrors_ref[...], preferred_element_type=jnp.float32
                ).astype(s_ref.dtype)
            for h in range(hb):
                dest = h if side == 0 else nband - 1 - h
                s_ref[g, dest] = joined[h * lines : (h + 1) * lines]
        for d in range(1, nband):
            homeward(g, d).start()
        cross(g, 0).start()
        o_ref[g, 0, band] = s_ref[g, band]

    def pass_on(g):
        for d in range(1, nband):
            homeward(g, d).wait_recv()
            cross(g, d).start()

    def synthesise_longitudes(g):
        for d in range(nband):
            cross(g, d).wait_recv()
        waves = 2 * nband * lines
        table = t_ref[g].reshape(waves, nlon)
        for q in range(0, rows, LANES):
            field_ref[q : q + LANES] += lax.dot_general(
                o_ref[g, :, :, :, q : q + LANES].reshape(waves, LANES), table, down,
                preferred_element_type=jnp.float32,
            )

    stages = (analyse_longitudes, analyse_latitudes, synthesise, pass_on, synthesise_longitudes)

    @pl.loop(0, groups + len(stages) - 1)
    def _(t):
        for late, stage in enumerate(stages):
            @pl.when((t >= late) & (t < groups + late))
            def _():
                stage(t - late)

    edge(0).wait_recv()
    edge(1).wait_recv()
    column().wait_recv()
    af_ref[...] = around_ref[...].astype(jnp.float32)
    r16 = lax.broadcasted_iota(jnp.int32, (16, LANES), 0)
    c16 = lax.broadcasted_iota(jnp.int32, (16, LANES), 1)
    place = ((r16 == 0) & (c16 == LANES - 1)) | ((r16 == 1) & (c16 == 0))
    we_ref[...] = lax.dot_general(
        side_ref[...], jnp.where(place, 1.0, 0.0).astype(jnp.bfloat16), down,
        preferred_element_type=jnp.float32,
    )
    step = 16
    scale = 1.0 / (2 * nlon)
    at = lax.broadcasted_iota(jnp.int32, (step, nlon), 1)

    @pl.loop(0, npop)
    def _(i):
        gain, thresh, decay, lateral = (par_ref[k, i] for k in range(4))
        base = pl.multiple_of(i * nlat, step)
        pad_ref[pl.ds(8, nlat)] = rates_ref[pl.ds(base, nlat)].astype(jnp.float32)
        pad_ref[7:8] = jnp.where(band > 0, af_ref[0, pl.ds(i, 1)], 0.0)
        pad_ref[8 + nlat : 9 + nlat] = jnp.where(band < nband - 1, af_ref[1, pl.ds(i, 1)], 0.0)
        for r in range(0, nlat, step):
            here = pl.ds(base + r, step)
            own = pad_ref[8 + r : 8 + r + step]
            ends = we_ref[here]
            beside = (
                jnp.where(at == 0, ends[:, LANES - 1 :], pltpu.roll(own, 1, 1))
                + jnp.where(at == nlon - 1, ends[:, :1], pltpu.roll(own, nlon - 1, 1))
                + pad_ref[9 + r : 9 + r + step]
                + pad_ref[7 + r : 7 + r + step]
                - 4.0 * own
            )
            u = u_ref[here]
            forcing = (
                -decay * u + field_ref[here] * scale + lateral * beside
                + drive_ref[here].astype(jnp.float32)
            )
            u = u + time_step * forcing
            un_ref[here] = u
            if not last:
                rn_ref[here] = jax.nn.sigmoid(gain * (u - thresh)).astype(rn_ref.dtype)

    edge(0).wait_send()
    edge(1).wait_send()
    column().wait_send()

    @pl.loop(0, groups)
    def _(g):
        partial(g).wait_send()
        swap(g).wait_send()
        for d in range(1, nband):
            outward(g, d).wait_send()
            homeward(g, d).wait_send()
        for d in range(nband):
            cross(g, d).wait_send()


def one_step(rates, table, mirror, mirrors, weights, basis, by_kind, kernels, u, drive, params,
             nband, npop, last):
    rows, nlon = rates.shape
    owned, half_lat, deg = basis.shape
    nlat = rows // npop
    groups = table.shape[0]
    group = owned // groups
    half = 2 * npop
    tiles = pl.cdiv(half_lat, LANES)
    dma = pltpu.SemaphoreType.DMA
    vmem = pl.BlockSpec(memory_space=pltpu.VMEM)
    hbm = pl.BlockSpec(memory_space=pltpu.MemorySpace.HBM)
    shapes = [jax.ShapeDtypeStruct(u.shape, jnp.float32)]
    if not last:
        shapes.append(jax.ShapeDtypeStruct(rates.shape, jnp.bfloat16))
    bf16 = jnp.bfloat16
    blocks = (groups, nband, 2 * group, rows)
    waves = nband * 2 * group
    return pl.pallas_call(
        functools.partial(step_kernel, nband, last),
        out_shape=tuple(shapes),
        in_specs=[vmem] * 5 + [hbm] + [vmem] * 4 + [pl.BlockSpec(memory_space=pltpu.SMEM)],
        out_specs=(vmem,) * len(shapes),
        scratch_shapes=[
            pltpu.VMEM((rows, nlon), bf16),
            pltpu.VMEM((groups, waves, rows), bf16),
            pltpu.VMEM((groups, waves, rows), bf16),
            pltpu.VMEM(blocks, bf16),
            pltpu.VMEM(blocks, bf16),
            pltpu.VMEM(basis.shape, bf16),
            pltpu.VMEM((owned, half, deg), bf16),
            pltpu.VMEM((owned, half, deg), bf16),
            pltpu.VMEM((tiles, group * 2 * half, LANES), jnp.float32),
            pltpu.VMEM((tiles, group * 2 * half, LANES), jnp.float32),
            pltpu.VMEM(blocks, bf16),
            pltpu.VMEM((groups, 2) + blocks[1:], bf16),
            pltpu.VMEM((rows, nlon), jnp.float32),
            pltpu.VMEM((nlat + 16, nlon), jnp.float32),
            pltpu.VMEM((2, 16, nlon), bf16),
            pltpu.VMEM((2, 16, nlon), bf16),
            pltpu.VMEM((2, 16, nlon), jnp.float32),
            pltpu.VMEM((16, rows), bf16),
            pltpu.VMEM((16, rows), bf16),
            pltpu.VMEM((rows, LANES), jnp.float32),
            dma((groups,)),
            dma((groups,)), dma((groups,)),
            dma((groups, nband - 1)), dma((groups, nband - 1)),
            dma((groups,)), dma((groups,)),
            dma((groups, nband - 1)), dma((groups, nband - 1)),
            dma((groups, nband)), dma((groups, nband)),
            dma((3,)), dma((3,)),
        ],
        compiler_params=pltpu.CompilerParams(
            collective_id=1 if last else 0, has_side_effects=True, vmem_limit_bytes=60 * 2**20
        ),
        name="last_step" if last else "one_step",
    )(rates, table, mirror, mirrors, weights, basis, by_kind, kernels, u, drive, params)


def wave_table(starts, owned, longitude, period):
    coarse = starts[:, None] + 16 * jnp.arange(owned // 16, dtype=jnp.int32)[None, :]
    fine = jnp.arange(16, dtype=jnp.int32)

    def angles(wave):
        phase = wave[..., None] * longitude % period
        angle = phase.astype(jnp.float32) * (2.0 * math.pi / period)
        return lax.optimization_barrier((jnp.cos(angle), jnp.sin(angle)))

    cos_a, sin_a = (v[:, :, None, :] for v in angles(coarse))
    cos_b, sin_b = (v[None, None, :, :] for v in angles(fine))
    shape = (starts.shape[0], owned, longitude.shape[0])
    cosine = (cos_a * cos_b - sin_a * sin_b).reshape(shape)
    sine = (sin_a * cos_b + cos_a * sin_b).reshape(shape)
    return jnp.stack([cosine, sine], axis=1)


def fast_local(activity, drive, basis, kernels, conn_block, coupling, rate_params):
    npop, nlat, nlon = activity.shape
    owned, half_lat, deg = basis.shape
    nband = lax.axis_size("band")
    hb = nband // 2
    period = nlon * lax.axis_size("lon")
    rows = npop * nlat
    band, lon, pop = lax.axis_index("band"), lax.axis_index("lon"), lax.axis_index("pop")
    pop_first = pop * npop
    params = lax.dynamic_slice_in_dim(rate_params, pop_first, npop, 1)
    gain_row, thresh = params[0, :, None, None], params[1, :, None, None]

    bands = jnp.arange(nband, dtype=jnp.int32)
    kk = jnp.arange(nlon, dtype=jnp.int32)
    own_start = (bands * 2 + lon) * owned
    other_start = (bands * 2 + 1 - lon) * owned
    starts = jnp.concatenate([own_start, other_start])
    table = wave_table(starts, owned, lon * nlon + kk, period).astype(jnp.bfloat16)
    table = table.reshape(2, nband, 2, owned // 16, 16, nlon).transpose(3, 0, 1, 2, 4, 5)
    table = table.reshape(owned // 16, 2, nband * 32, nlon)

    row_index = jnp.arange(half_lat, dtype=jnp.float32)
    colatitude = math.pi * (4.0 * row_index + 3.0) / (8.0 * half_lat + 2.0)
    weights = math.pi * jnp.sin(colatitude) / (2.0 * half_lat)
    weights = jnp.tile(weights.reshape(hb, 1, nlat), (1, 1, npop))

    south = band >= hb
    lat = jnp.arange(nlat, dtype=jnp.int32)
    mirror = (lat[:, None] == jnp.where(south, nlat - 1 - lat, lat)[None, :]).astype(jnp.bfloat16)
    back = (lat[:, None] == nlat - 1 - lat[None, :]).astype(jnp.bfloat16)
    mirrors = jnp.einsum("xy,ab->xayb", jnp.eye(npop, dtype=jnp.bfloat16), back)
    mirrors = mirrors.reshape(rows, rows)

    coup_own = lax.dynamic_slice_in_dim(coupling, pop_first, npop, 0)
    block_own = lax.dynamic_slice_in_dim(conn_block, pop_first, npop, 0)
    kind = jnp.arange(kernels.shape[0], dtype=jnp.int32)
    per_kind = jnp.where(block_own[None] == kind[:, None, None], coup_own[None], 0.0)
    per_kind = jnp.concatenate(
        [
            lax.dynamic_slice_in_dim(per_kind, pop_first, npop, 2),
            lax.dynamic_slice_in_dim(per_kind, (1 - pop) * npop, npop, 2),
        ],
        axis=2,
    )
    spread = per_kind[:, :, None, :, None] * jnp.eye(2, dtype=jnp.float32)[:, None, :]
    spread = spread.reshape(kernels.shape[0] * npop * 2, 2 * npop * 2)
    coarse = lax.reduce_precision(spread, 8, 7)
    by_kind = jnp.concatenate([coarse, spread - coarse], axis=1).astype(jnp.bfloat16)

    drive = drive.reshape(rows, nlon)
    u = activity.reshape(rows, nlon)
    rates = jax.nn.sigmoid(gain_row * (activity - thresh)).astype(jnp.bfloat16)
    rates = rates.reshape(rows, nlon)
    for step_index in range(STEPS):
        last = step_index == STEPS - 1
        results = one_step(
            rates, table, mirror, mirrors, weights, basis, by_kind, kernels, u, drive, params,
            nband, npop, last,
        )
        if last:
            (u,) = results
        else:
            u, rates = results
    return u.reshape(npop, nlat, nlon)


def dispatch(activity, drive, basis, *rest):
    npop, nlat, nlon = activity.shape
    owned, half_lat, deg = basis.shape
    fits = (
        lax.axis_size("lon") == 2
        and lax.axis_size("pop") == 2
        and lax.axis_size("band") % 2 == 0
        and npop == 4
        and owned % 16 == 0
        and nlat % 16 == 0
        and (npop * nlat) % LANES == 0
        and nlon % LANES == 0
        and deg % LANES == 0
        and 2 * basis.size <= 40 * 2**20
    )
    return (fast_local if fits else local)(activity, drive, basis, *rest)


def solution(mesh):
    in_specs = (
        P(("subj", "pop"), "band", "lon"),
        P(("subj", "pop"), "band", "lon"),
        P(("subj", "band", "lon"), None, None),
        P(),
        P(),
        P("subj", None),
        P("subj", None),
    )
    out_specs = P(("subj", "pop"), "band", "lon")
    return jax.shard_map(
        dispatch, mesh=mesh, in_specs=in_specs, out_specs=out_specs, check_vma=False
    )
```

```python
import functools
import math

import jax
import jax.numpy as jnp
from jax import lax
from jax.experimental import pallas as pl
from jax.experimental.pallas import tpu as pltpu
from jax.sharding import PartitionSpec as P

NLAT = 640
NLON = 1280
DEG = 640
STEPS = 2


time_step = 0.5


def with_halo(shard, sides, width):
    for axis, dim in sides:
        size, length = (lax.axis_size(axis), shard.shape[dim])
        up = [(i, (i + 1) % size) for i in range(size - 1)]
        down = [(j, i) for i, j in up]
        last = lax.slice_in_dim(shard, length - width, length, axis=dim)
        leading = lax.slice_in_dim(shard, 0, width, axis=dim)
        before = lax.ppermute(last, axis, up)
        after = lax.ppermute(leading, axis, down)
        shard = jnp.concatenate([before, shard, after], axis=dim)
    return shard


def fourier_table():
    longitude = jnp.arange(NLON, dtype=jnp.int32)
    wavenumber = jnp.arange(DEG, dtype=jnp.int32)
    phase = longitude[:, None] * wavenumber[None, :] % NLON
    angle = phase.astype(jnp.float32) * (2.0 * math.pi / NLON)
    return jnp.stack([jnp.cos(angle), jnp.sin(angle)], axis=1).astype(jnp.bfloat16)


def lat_weights():
    row_index = jnp.arange(NLAT // 2, dtype=jnp.float32)
    colatitude = math.pi * (4.0 * row_index + 3.0) / (4.0 * NLAT + 2.0)
    return math.pi * jnp.sin(colatitude) / NLAT


def to_owners(fourier):
    return lax.all_to_all(fourier, ("band", "lon"), split_axis=2, concat_axis=3, tiled=True)


def to_latitudes(synthesis):
    return lax.all_to_all(synthesis, ("band", "lon"), split_axis=3, concat_axis=2, tiled=True)


def local(activity, drive, basis, kernels, conn_block, coupling, rate_params):
    pop_here = activity.shape[0]
    owned_count = basis.shape[0]
    half_lat = basis.shape[1]
    quarter = DEG // 2
    owner_index = lax.axis_index("band") * lax.axis_size("lon") + lax.axis_index("lon")
    pop_first = lax.axis_index("pop") * pop_here
    params = lax.dynamic_slice_in_dim(rate_params, pop_first, pop_here, 1)
    gain_row, thresh, decay_row, lateral = (params[0], params[1], params[2], params[3])
    cos_sin = fourier_table()
    weights = lat_weights()
    wavenumber = owner_index * owned_count + jnp.arange(owned_count, dtype=jnp.int32)
    degree = jnp.arange(DEG, dtype=jnp.int32)
    triangle = degree[None, :] >= wavenumber[:, None]
    slots = jnp.arange(2, dtype=jnp.int32)
    parity_pick = (slots[None, :] == (wavenumber % 2)[:, None])[None, None, :, :, None]
    every_wave = jnp.arange(DEG, dtype=jnp.int32)
    amplitude = jnp.where(every_wave == 0, 1.0, 2.0).astype(jnp.bfloat16)
    coup_own = lax.dynamic_slice_in_dim(coupling, pop_first, pop_here, 0)
    block_own = lax.dynamic_slice_in_dim(conn_block, pop_first, pop_here, 0)
    onehot = (block_own[..., None] == jnp.arange(kernels.shape[0], dtype=jnp.int32)).astype(
        jnp.float32
    )
    mixing = coup_own[..., None] * jnp.einsum(
        "ijb,bn->ijn", onehot, kernels, precision=lax.Precision.HIGHEST
    )
    basis_split = basis.reshape(owned_count, half_lat, quarter, 2)
    drive_f32 = drive.astype(jnp.float32)
    activity_now = activity
    for step_index in range(STEPS):
        rates = jax.nn.sigmoid(
            gain_row[:, None, None] * (activity_now - thresh[:, None, None])
        ).astype(jnp.bfloat16)
        lat_rows = lax.all_to_all(rates, "lon", split_axis=1, concat_axis=2, tiled=True)
        fourier = jnp.einsum(
            "ijk,kcm->icmj", lat_rows, cos_sin, preferred_element_type=jnp.float32
        ).astype(jnp.bfloat16)
        spectrum = to_owners(fourier)
        northern = spectrum[..., :half_lat].astype(jnp.float32)
        southern = jnp.flip(spectrum[..., half_lat:], axis=3).astype(jnp.float32)
        even_part = (weights * (northern + southern)).astype(jnp.bfloat16)
        odd_part = (weights * (northern - southern)).astype(jnp.bfloat16)
        operand = jnp.where(parity_pick, even_part[:, :, :, None, :], odd_part[:, :, :, None, :])
        coeffs = jnp.einsum(
            "icmsj,mjqs->icmqs", operand, basis_split, preferred_element_type=jnp.float32
        )
        coeffs = coeffs.reshape(pop_here, 2, owned_count, DEG)
        coeffs = jnp.where(triangle[None, None], coeffs, 0.0)
        gathered = lax.all_gather(coeffs.astype(jnp.bfloat16), "pop", axis=0, tiled=True).astype(
            coeffs.dtype
        )
        mixed_spec = jnp.sum(mixing[:, :, None, None, :] * gathered[None], axis=1).astype(
            jnp.bfloat16
        )
        degree_parts = jnp.einsum(
            "icmqs,mjqs->icmsj",
            mixed_spec.reshape(pop_here, 2, owned_count, quarter, 2),
            basis_split,
            preferred_element_type=jnp.float32,
        )
        same_parity = jnp.sum(jnp.where(parity_pick, degree_parts, 0.0), axis=3)
        other_parity = jnp.sum(jnp.where(parity_pick, 0.0, degree_parts), axis=3)
        synthesis = jnp.concatenate(
            [same_parity + other_parity, jnp.flip(same_parity - other_parity, axis=3)], axis=3
        ).astype(jnp.bfloat16)
        returned = to_latitudes(synthesis)
        scaled = returned * amplitude[None, None, :, None]
        synth_field = jnp.einsum(
            "icmj,kcm->ijk", scaled, cos_sin, preferred_element_type=jnp.float32
        ) * (1.0 / NLON)
        padded = with_halo(lat_rows, ((("band", "lon"), 1),), 1).astype(jnp.float32)
        rates_f32 = lat_rows.astype(jnp.float32)
        lateral_term = (
            jnp.roll(rates_f32, 1, axis=2)
            + jnp.roll(rates_f32, -1, axis=2)
            + padded[:, 2:, :]
            + padded[:, :-2, :]
            - 4.0 * rates_f32
        )
        coupled = synth_field + lateral[:, None, None] * lateral_term
        coupled_grid = lax.all_to_all(
            coupled.astype(jnp.bfloat16), "lon", split_axis=2, concat_axis=1, tiled=True
        ).astype(coupled.dtype)
        forcing = -decay_row[:, None, None] * activity_now + coupled_grid + drive_f32
        activity_now = activity_now + time_step * forcing
    return activity_now


MESH = pl.DeviceIdType.MESH
LANES = 128


def remote(src, dst, send_sem, recv_sem, peer):
    return pltpu.make_async_remote_copy(
        src_ref=src, dst_ref=dst, send_sem=send_sem, recv_sem=recv_sem,
        device_id=peer, device_id_type=MESH,
    )


def step_kernel(nband, t_ref, mirror_ref, mirrors_ref, w_ref, b_hbm, a_ref, k_ref,
                u_ref, drive_ref, par_ref, un_ref, *rest):
    (rates_ref, face_ref, ps_ref, pr_ref, fz_ref, gz_ref, b_ref, own_ref, other_ref, x_ref, y_ref, s_ref, o_ref,
     field_ref, pad_ref, edge_ref, around_ref, af_ref, col_ref, side_ref, we_ref,
     bsem, ps, pr, zs, zr, ss, rs, ys, yr, xs, xr, es, er) = rest
    band, lon = lax.axis_index("band"), lax.axis_index("lon")
    rows, nlon = rates_ref.shape
    owned, half_lat, deg = b_ref.shape
    groups = t_ref.shape[0]
    group = owned // groups
    half = own_ref.shape[1]
    both = 2 * half
    npop = half // 2
    hb = nband // 2
    nlat = half_lat // hb
    lines = 2 * group
    first = (band * lax.axis_size("lon") + lon) * owned
    kinds = k_ref.shape[0]
    across = {"lon": 1 - lon}
    mate = {"pop": 1 - lax.axis_index("pop")}
    tiles = x_ref.shape[0]
    spare = tiles * LANES - half_lat
    padding = [jnp.zeros((group, spare), jnp.float32)] if spare else []
    wide_padding = [jnp.zeros((both, spare), jnp.float32)] if spare else []
    degree = lax.broadcasted_iota(jnp.int32, (half, deg), 1)
    along = (((1,), (1,)), ((), ()))
    down = (((0,), (0,)), ((), ()))

    def forward_band(d):
        return lax.rem(band + d, nband)

    def backward_band(d):
        return lax.rem(band + nband - d, nband)

    def fetch(g):
        part = pl.ds(g * group, group)
        return pltpu.make_async_copy(b_hbm.at[part], b_ref.at[part], bsem.at[g])

    def partial(g):
        return remote(ps_ref.at[g], pr_ref.at[g], ps.at[g], pr.at[g], across)

    def outward(g, d):
        dest = forward_band(d)
        return remote(
            fz_ref.at[g, dest], gz_ref.at[g, band], zs.at[g, d - 1], zr.at[g, d - 1], {"band": dest}
        )

    def swap(g):
        part = pl.ds(g * group, group)
        return remote(own_ref.at[part], other_ref.at[part], ss.at[g], rs.at[g], mate)

    def homeward(g, d):
        dest = forward_band(d)
        return remote(
            s_ref.at[g, dest], o_ref.at[g, 0, band], ys.at[g, d - 1], yr.at[g, d - 1], {"band": dest}
        )

    def cross(g, d):
        source = backward_band(d)
        block = s_ref.at[g, band] if d == 0 else o_ref.at[g, 0, source]
        return remote(block, o_ref.at[g, 1, source], xs.at[g, d], xr.at[g, d], across)

    def edge(side):
        peer = {"band": forward_band(1 if side == 0 else nband - 1)}
        return remote(edge_ref.at[side], around_ref.at[side], es.at[side], er.at[side], peer)

    def column():
        return remote(col_ref, side_ref, es.at[2], er.at[2], across)

    @pl.loop(0, groups)
    def _(g):
        fetch(g).start()

    barrier = pltpu.get_barrier_semaphore()
    for d in range(1, nband):
        peer = {"band": forward_band(d)}
        pl.semaphore_signal(barrier, inc=1, device_id=peer, device_id_type=MESH)
    pl.semaphore_signal(barrier, inc=1, device_id=across, device_id_type=MESH)
    pl.semaphore_signal(barrier, inc=1, device_id=mate, device_id_type=MESH)

    @pl.loop(0, npop)
    def _(i):
        gain, thresh = par_ref[0, i], par_ref[1, i]
        for r in range(0, nlat, 16):
            here = pl.ds(pl.multiple_of(i * nlat + r, 16), 16)
            rates_ref[here] = jax.nn.sigmoid(gain * (u_ref[here] - thresh)).astype(rates_ref.dtype)
        part = pl.ds(pl.multiple_of(i * nlat, 16), nlat)
        face_ref[part] = jnp.dot(
            mirror_ref[...], rates_ref[part], preferred_element_type=jnp.float32
        ).astype(face_ref.dtype)
    pl.semaphore_wait(barrier, nband + 1)

    @pl.loop(0, groups)
    def _(g):
        ps_ref[g] = lax.dot_general(
            t_ref[g, 1], face_ref[...], along, preferred_element_type=jnp.float32
        ).astype(ps_ref.dtype)
        partial(g).start()

    fill = jnp.zeros((16 - npop, nlon), jnp.float32)
    for side, at in ((0, nlat - 1), (1, 0)):
        picked = [
            rates_ref[i * nlat + at : i * nlat + at + 1].astype(jnp.float32) for i in range(npop)
        ]
        edge_ref[side] = jnp.concatenate(picked + [fill], axis=0).astype(edge_ref.dtype)
    r16 = lax.broadcasted_iota(jnp.int32, (16, nlon), 0)
    c16 = lax.broadcasted_iota(jnp.int32, (16, nlon), 1)
    pick = ((r16 == 0) & (c16 == nlon - 1)) | ((r16 == 1) & (c16 == 0))
    col_ref[...] = lax.dot_general(
        jnp.where(pick, 1.0, 0.0).astype(jnp.bfloat16), rates_ref[...], along,
        preferred_element_type=jnp.float32,
    ).astype(col_ref.dtype)
    edge(0).start()
    edge(1).start()
    column().start()
    field_ref[...] = jnp.zeros_like(field_ref)

    def analyse_longitudes(g):
        total = lax.dot_general(
            t_ref[g, 0], face_ref[...], along, preferred_element_type=jnp.float32
        )
        partial(g).wait_recv()
        total = (total + pr_ref[g].astype(jnp.float32)).astype(fz_ref.dtype)
        fz_ref[g] = total.reshape(fz_ref.shape[1:])
        for d in range(1, nband):
            outward(g, d).start()
        gz_ref[g, band] = fz_ref[g, band]

    def analyse_latitudes(g):
        for d in range(1, nband):
            outward(g, d).wait_recv()
        for cc in range(2):
            part = slice(cc * group, (cc + 1) * group)
            parts = []
            for h in range(hb):
                north = gz_ref[g, h, part, :].astype(jnp.float32)
                south = gz_ref[g, nband - 1 - h, part, :].astype(jnp.float32)
                parts.append((w_ref[h] * (north + south), w_ref[h] * (north - south)))
            for side in range(2):
                for i in range(npop):
                    row = side * half + i * 2 + cc
                    line = [piece[side][:, i * nlat : (i + 1) * nlat] for piece in parts]
                    line = jnp.concatenate(line + padding, axis=1)
                    for t in range(tiles):
                        x_ref[t, pl.ds(row, group, stride=both), :] = line[
                            :, t * LANES : (t + 1) * LANES
                        ]
        fetch(g).wait()
        for k in range(group):
            m = g * group + k
            x = [x_ref[t, k * both : (k + 1) * both, :] for t in range(tiles)]
            x = jnp.concatenate(x, axis=1)[:, :half_lat].astype(jnp.bfloat16)
            parity = jnp.dot(x, b_ref[m], preferred_element_type=jnp.float32)
            gap = degree - (first + m)
            coeffs = jnp.where(gap % 2 == 0, parity[:half], parity[half:])
            own_ref[m] = jnp.where(gap >= 0, coeffs, 0.0).astype(own_ref.dtype)
        swap(g).start()

    def synthesise(g):
        swap(g).wait_recv()
        for k in range(group):
            m = g * group + k
            pair = jnp.concatenate(
                [own_ref[m].astype(jnp.float32), other_ref[m].astype(jnp.float32)], axis=0
            ).astype(jnp.bfloat16)
            by_kind = jnp.dot(
                a_ref[...], jnp.concatenate([pair, pair], axis=0),
                preferred_element_type=jnp.float32,
            )
            mixed = k_ref[0:1] * by_kind[:half]
            for kind in range(1, kinds):
                mixed += k_ref[kind : kind + 1] * by_kind[kind * half : (kind + 1) * half]
            gap = degree - (first + m)
            signed = jnp.where(gap % 2 == 0, mixed, -mixed)
            y = lax.dot_general(
                jnp.concatenate([mixed, signed], axis=0).astype(jnp.bfloat16), b_ref[m],
                along, preferred_element_type=jnp.float32,
            )
            y = y * jnp.where(first + m == 0, 1.0, 2.0)
            y = jnp.concatenate([y] + wide_padding, axis=1)
            for t in range(tiles):
                y_ref[t, k * both : (k + 1) * both, :] = y[:, t * LANES : (t + 1) * LANES]
        for side in range(2):
            blocks = [[None, None] for h in range(hb)]
            for cc in range(2):
                wide = [
                    jnp.concatenate(
                        [
                            y_ref[t, pl.ds(side * half + i * 2 + cc, group, stride=both), :]
                            for t in range(tiles)
                        ],
                        axis=1,
                    )
                    for i in range(npop)
                ]
                for h in range(hb):
                    blocks[h][cc] = jnp.concatenate(
                        [row[:, h * nlat : (h + 1) * nlat] for row in wide], axis=1
                    ).astype(s_ref.dtype)
            joined = jnp.concatenate([piece for block in blocks for piece in block], axis=0)
            if side == 1:
                joined = jnp.dot(
                    joined, mirrors_ref[...], preferred_element_type=jnp.float32
                ).astype(s_ref.dtype)
            for h in range(hb):
                dest = h if side == 0 else nband - 1 - h
                s_ref[g, dest] = joined[h * lines : (h + 1) * lines]
        for d in range(1, nband):
            homeward(g, d).start()
        cross(g, 0).start()
        o_ref[g, 0, band] = s_ref[g, band]

    def pass_on(g):
        for d in range(1, nband):
            homeward(g, d).wait_recv()
            cross(g, d).start()

    def synthesise_longitudes(g):
        for d in range(nband):
            cross(g, d).wait_recv()
        waves = 2 * nband * lines
        table = t_ref[g].reshape(waves, nlon)
        for q in range(0, rows, LANES):
            field_ref[q : q + LANES] += lax.dot_general(
                o_ref[g, :, :, :, q : q + LANES].reshape(waves, LANES), table, down,
                preferred_element_type=jnp.float32,
            )

    stages = (analyse_longitudes, analyse_latitudes, synthesise, pass_on, synthesise_longitudes)

    @pl.loop(0, groups + len(stages) - 1)
    def _(t):
        for late, stage in enumerate(stages):
            @pl.when((t >= late) & (t < groups + late))
            def _():
                stage(t - late)

    edge(0).wait_recv()
    edge(1).wait_recv()
    column().wait_recv()
    af_ref[...] = around_ref[...].astype(jnp.float32)
    r16 = lax.broadcasted_iota(jnp.int32, (16, LANES), 0)
    c16 = lax.broadcasted_iota(jnp.int32, (16, LANES), 1)
    place = ((r16 == 0) & (c16 == LANES - 1)) | ((r16 == 1) & (c16 == 0))
    we_ref[...] = lax.dot_general(
        side_ref[...], jnp.where(place, 1.0, 0.0).astype(jnp.bfloat16), down,
        preferred_element_type=jnp.float32,
    )
    step = 16
    scale = 1.0 / (2 * nlon)
    at = lax.broadcasted_iota(jnp.int32, (step, nlon), 1)

    @pl.loop(0, npop)
    def _(i):
        decay, lateral = par_ref[2, i], par_ref[3, i]
        base = pl.multiple_of(i * nlat, step)
        pad_ref[pl.ds(8, nlat)] = rates_ref[pl.ds(base, nlat)].astype(jnp.float32)
        pad_ref[7:8] = jnp.where(band > 0, af_ref[0, pl.ds(i, 1)], 0.0)
        pad_ref[8 + nlat : 9 + nlat] = jnp.where(band < nband - 1, af_ref[1, pl.ds(i, 1)], 0.0)
        for r in range(0, nlat, step):
            here = pl.ds(base + r, step)
            own = pad_ref[8 + r : 8 + r + step]
            ends = we_ref[here]
            beside = (
                jnp.where(at == 0, ends[:, LANES - 1 :], pltpu.roll(own, 1, 1))
                + jnp.where(at == nlon - 1, ends[:, :1], pltpu.roll(own, nlon - 1, 1))
                + pad_ref[9 + r : 9 + r + step]
                + pad_ref[7 + r : 7 + r + step]
                - 4.0 * own
            )
            u = u_ref[here]
            forcing = (
                -decay * u + field_ref[here] * scale + lateral * beside
                + drive_ref[here].astype(jnp.float32)
            )
            un_ref[here] = u + time_step * forcing

    edge(0).wait_send()
    edge(1).wait_send()
    column().wait_send()

    @pl.loop(0, groups)
    def _(g):
        partial(g).wait_send()
        swap(g).wait_send()
        for d in range(1, nband):
            outward(g, d).wait_send()
            homeward(g, d).wait_send()
        for d in range(nband):
            cross(g, d).wait_send()


def one_step(table, mirror, mirrors, weights, basis, by_kind, kernels, u, drive, params,
             nband, npop, last):
    rows, nlon = u.shape
    owned, half_lat, deg = basis.shape
    nlat = rows // npop
    groups = table.shape[0]
    group = owned // groups
    half = 2 * npop
    tiles = pl.cdiv(half_lat, LANES)
    dma = pltpu.SemaphoreType.DMA
    vmem = pl.BlockSpec(memory_space=pltpu.VMEM)
    hbm = pl.BlockSpec(memory_space=pltpu.MemorySpace.HBM)
    bf16 = jnp.bfloat16
    blocks = (groups, nband, 2 * group, rows)
    waves = nband * 2 * group
    return pl.pallas_call(
        functools.partial(step_kernel, nband),
        out_shape=jax.ShapeDtypeStruct(u.shape, jnp.float32),
        in_specs=[vmem] * 4 + [hbm] + [vmem] * 4 + [pl.BlockSpec(memory_space=pltpu.SMEM)],
        out_specs=vmem,
        scratch_shapes=[
            pltpu.VMEM((rows, nlon), bf16),
            pltpu.VMEM((rows, nlon), bf16),
            pltpu.VMEM((groups, waves, rows), bf16),
            pltpu.VMEM((groups, waves, rows), bf16),
            pltpu.VMEM(blocks, bf16),
            pltpu.VMEM(blocks, bf16),
            pltpu.VMEM(basis.shape, bf16),
            pltpu.VMEM((owned, half, deg), bf16),
            pltpu.VMEM((owned, half, deg), bf16),
            pltpu.VMEM((tiles, group * 2 * half, LANES), jnp.float32),
            pltpu.VMEM((tiles, group * 2 * half, LANES), jnp.float32),
            pltpu.VMEM(blocks, bf16),
            pltpu.VMEM((groups, 2) + blocks[1:], bf16),
            pltpu.VMEM((rows, nlon), jnp.float32),
            pltpu.VMEM((nlat + 16, nlon), jnp.float32),
            pltpu.VMEM((2, 16, nlon), bf16),
            pltpu.VMEM((2, 16, nlon), bf16),
            pltpu.VMEM((2, 16, nlon), jnp.float32),
            pltpu.VMEM((16, rows), bf16),
            pltpu.VMEM((16, rows), bf16),
            pltpu.VMEM((rows, LANES), jnp.float32),
            dma((groups,)),
            dma((groups,)), dma((groups,)),
            dma((groups, nband - 1)), dma((groups, nband - 1)),
            dma((groups,)), dma((groups,)),
            dma((groups, nband - 1)), dma((groups, nband - 1)),
            dma((groups, nband)), dma((groups, nband)),
            dma((3,)), dma((3,)),
        ],
        compiler_params=pltpu.CompilerParams(
            collective_id=1 if last else 0, has_side_effects=True, vmem_limit_bytes=60 * 2**20
        ),
        name="last_step" if last else "one_step",
    )(table, mirror, mirrors, weights, basis, by_kind, kernels, u, drive, params)


def wave_table(starts, owned, longitude, period):
    coarse = starts[:, None] + 16 * jnp.arange(owned // 16, dtype=jnp.int32)[None, :]
    fine = jnp.arange(16, dtype=jnp.int32)

    def angles(wave):
        phase = wave[..., None] * longitude % period
        angle = phase.astype(jnp.float32) * (2.0 * math.pi / period)
        return lax.optimization_barrier((jnp.cos(angle), jnp.sin(angle)))

    cos_a, sin_a = (v[:, :, None, :] for v in angles(coarse))
    cos_b, sin_b = (v[None, None, :, :] for v in angles(fine))
    shape = (starts.shape[0], owned, longitude.shape[0])
    cosine = (cos_a * cos_b - sin_a * sin_b).reshape(shape)
    sine = (sin_a * cos_b + cos_a * sin_b).reshape(shape)
    return jnp.stack([cosine, sine], axis=1)


def fast_local(activity, drive, basis, kernels, conn_block, coupling, rate_params):
    npop, nlat, nlon = activity.shape
    owned, half_lat, deg = basis.shape
    nband = lax.axis_size("band")
    hb = nband // 2
    period = nlon * lax.axis_size("lon")
    rows = npop * nlat
    band, lon, pop = lax.axis_index("band"), lax.axis_index("lon"), lax.axis_index("pop")
    pop_first = pop * npop
    params = lax.dynamic_slice_in_dim(rate_params, pop_first, npop, 1)

    bands = jnp.arange(nband, dtype=jnp.int32)
    kk = jnp.arange(nlon, dtype=jnp.int32)
    own_start = (bands * 2 + lon) * owned
    other_start = (bands * 2 + 1 - lon) * owned
    starts = jnp.concatenate([own_start, other_start])
    table = wave_table(starts, owned, lon * nlon + kk, period).astype(jnp.bfloat16)
    table = table.reshape(2, nband, 2, owned // 16, 16, nlon).transpose(3, 0, 1, 2, 4, 5)
    table = table.reshape(owned // 16, 2, nband * 32, nlon)

    row_index = jnp.arange(half_lat, dtype=jnp.float32)
    colatitude = math.pi * (4.0 * row_index + 3.0) / (8.0 * half_lat + 2.0)
    weights = math.pi * jnp.sin(colatitude) / (2.0 * half_lat)
    weights = jnp.tile(weights.reshape(hb, 1, nlat), (1, 1, npop))

    south = band >= hb
    lat = jnp.arange(nlat, dtype=jnp.int32)
    mirror = (lat[:, None] == jnp.where(south, nlat - 1 - lat, lat)[None, :]).astype(jnp.bfloat16)
    cell = jnp.arange(rows, dtype=jnp.int32)
    image = cell // nlat * nlat + (nlat - 1 - cell % nlat)
    mirrors = (cell[:, None] == image[None, :]).astype(jnp.bfloat16)

    coup_own = lax.dynamic_slice_in_dim(coupling, pop_first, npop, 0)
    block_own = lax.dynamic_slice_in_dim(conn_block, pop_first, npop, 0)
    kind = jnp.arange(kernels.shape[0], dtype=jnp.int32)
    per_kind = jnp.where(block_own[None] == kind[:, None, None], coup_own[None], 0.0)
    per_kind = jnp.concatenate(
        [
            lax.dynamic_slice_in_dim(per_kind, pop_first, npop, 2),
            lax.dynamic_slice_in_dim(per_kind, (1 - pop) * npop, npop, 2),
        ],
        axis=2,
    )
    spread = per_kind[:, :, None, :, None] * jnp.eye(2, dtype=jnp.float32)[:, None, :]
    spread = spread.reshape(kernels.shape[0] * npop * 2, 2 * npop * 2)
    coarse = lax.reduce_precision(spread, 8, 7)
    by_kind = jnp.concatenate([coarse, spread - coarse], axis=1).astype(jnp.bfloat16)

    drive = drive.reshape(rows, nlon)
    u = activity.reshape(rows, nlon)
    for step_index in range(STEPS):
        u = one_step(
            table, mirror, mirrors, weights, basis, by_kind, kernels, u, drive, params,
            nband, npop, step_index == STEPS - 1,
        )
    return u.reshape(npop, nlat, nlon)


def dispatch(activity, drive, basis, *rest):
    npop, nlat, nlon = activity.shape
    owned, half_lat, deg = basis.shape
    fits = (
        lax.axis_size("lon") == 2
        and lax.axis_size("pop") == 2
        and lax.axis_size("band") % 2 == 0
        and npop == 4
        and owned % 16 == 0
        and nlat % 16 == 0
        and (npop * nlat) % LANES == 0
        and nlon % LANES == 0
        and deg % LANES == 0
        and 2 * basis.size <= 40 * 2**20
    )
    return (fast_local if fits else local)(activity, drive, basis, *rest)


def solution(mesh):
    in_specs = (
        P(("subj", "pop"), "band", "lon"),
        P(("subj", "pop"), "band", "lon"),
        P(("subj", "band", "lon"), None, None),
        P(),
        P(),
        P("subj", None),
        P("subj", None),
    )
    out_specs = P(("subj", "pop"), "band", "lon")
    return jax.shard_map(
        dispatch, mesh=mesh, in_specs=in_specs, out_specs=out_specs, check_vma=False
    )
```

```python
import functools
import math

import jax
import jax.numpy as jnp
from jax import lax
from jax.experimental import pallas as pl
from jax.experimental.pallas import tpu as pltpu
from jax.sharding import PartitionSpec as P

NLAT = 640
NLON = 1280
DEG = 640
STEPS = 2


time_step = 0.5


def with_halo(shard, sides, width):
    for axis, dim in sides:
        size, length = (lax.axis_size(axis), shard.shape[dim])
        up = [(i, (i + 1) % size) for i in range(size - 1)]
        down = [(j, i) for i, j in up]
        last = lax.slice_in_dim(shard, length - width, length, axis=dim)
        leading = lax.slice_in_dim(shard, 0, width, axis=dim)
        before = lax.ppermute(last, axis, up)
        after = lax.ppermute(leading, axis, down)
        shard = jnp.concatenate([before, shard, after], axis=dim)
    return shard


def fourier_table():
    longitude = jnp.arange(NLON, dtype=jnp.int32)
    wavenumber = jnp.arange(DEG, dtype=jnp.int32)
    phase = longitude[:, None] * wavenumber[None, :] % NLON
    angle = phase.astype(jnp.float32) * (2.0 * math.pi / NLON)
    return jnp.stack([jnp.cos(angle), jnp.sin(angle)], axis=1).astype(jnp.bfloat16)


def lat_weights():
    row_index = jnp.arange(NLAT // 2, dtype=jnp.float32)
    colatitude = math.pi * (4.0 * row_index + 3.0) / (4.0 * NLAT + 2.0)
    return math.pi * jnp.sin(colatitude) / NLAT


def to_owners(fourier):
    return lax.all_to_all(fourier, ("band", "lon"), split_axis=2, concat_axis=3, tiled=True)


def to_latitudes(synthesis):
    return lax.all_to_all(synthesis, ("band", "lon"), split_axis=3, concat_axis=2, tiled=True)


def local(activity, drive, basis, kernels, conn_block, coupling, rate_params):
    pop_here = activity.shape[0]
    owned_count = basis.shape[0]
    half_lat = basis.shape[1]
    quarter = DEG // 2
    owner_index = lax.axis_index("band") * lax.axis_size("lon") + lax.axis_index("lon")
    pop_first = lax.axis_index("pop") * pop_here
    params = lax.dynamic_slice_in_dim(rate_params, pop_first, pop_here, 1)
    gain_row, thresh, decay_row, lateral = (params[0], params[1], params[2], params[3])
    cos_sin = fourier_table()
    weights = lat_weights()
    wavenumber = owner_index * owned_count + jnp.arange(owned_count, dtype=jnp.int32)
    degree = jnp.arange(DEG, dtype=jnp.int32)
    triangle = degree[None, :] >= wavenumber[:, None]
    slots = jnp.arange(2, dtype=jnp.int32)
    parity_pick = (slots[None, :] == (wavenumber % 2)[:, None])[None, None, :, :, None]
    every_wave = jnp.arange(DEG, dtype=jnp.int32)
    amplitude = jnp.where(every_wave == 0, 1.0, 2.0).astype(jnp.bfloat16)
    coup_own = lax.dynamic_slice_in_dim(coupling, pop_first, pop_here, 0)
    block_own = lax.dynamic_slice_in_dim(conn_block, pop_first, pop_here, 0)
    onehot = (block_own[..., None] == jnp.arange(kernels.shape[0], dtype=jnp.int32)).astype(
        jnp.float32
    )
    mixing = coup_own[..., None] * jnp.einsum(
        "ijb,bn->ijn", onehot, kernels, precision=lax.Precision.HIGHEST
    )
    basis_split = basis.reshape(owned_count, half_lat, quarter, 2)
    drive_f32 = drive.astype(jnp.float32)
    activity_now = activity
    for step_index in range(STEPS):
        rates = jax.nn.sigmoid(
            gain_row[:, None, None] * (activity_now - thresh[:, None, None])
        ).astype(jnp.bfloat16)
        lat_rows = lax.all_to_all(rates, "lon", split_axis=1, concat_axis=2, tiled=True)
        fourier = jnp.einsum(
            "ijk,kcm->icmj", lat_rows, cos_sin, preferred_element_type=jnp.float32
        ).astype(jnp.bfloat16)
        spectrum = to_owners(fourier)
        northern = spectrum[..., :half_lat].astype(jnp.float32)
        southern = jnp.flip(spectrum[..., half_lat:], axis=3).astype(jnp.float32)
        even_part = (weights * (northern + southern)).astype(jnp.bfloat16)
        odd_part = (weights * (northern - southern)).astype(jnp.bfloat16)
        operand = jnp.where(parity_pick, even_part[:, :, :, None, :], odd_part[:, :, :, None, :])
        coeffs = jnp.einsum(
            "icmsj,mjqs->icmqs", operand, basis_split, preferred_element_type=jnp.float32
        )
        coeffs = coeffs.reshape(pop_here, 2, owned_count, DEG)
        coeffs = jnp.where(triangle[None, None], coeffs, 0.0)
        gathered = lax.all_gather(coeffs.astype(jnp.bfloat16), "pop", axis=0, tiled=True).astype(
            coeffs.dtype
        )
        mixed_spec = jnp.sum(mixing[:, :, None, None, :] * gathered[None], axis=1).astype(
            jnp.bfloat16
        )
        degree_parts = jnp.einsum(
            "icmqs,mjqs->icmsj",
            mixed_spec.reshape(pop_here, 2, owned_count, quarter, 2),
            basis_split,
            preferred_element_type=jnp.float32,
        )
        same_parity = jnp.sum(jnp.where(parity_pick, degree_parts, 0.0), axis=3)
        other_parity = jnp.sum(jnp.where(parity_pick, 0.0, degree_parts), axis=3)
        synthesis = jnp.concatenate(
            [same_parity + other_parity, jnp.flip(same_parity - other_parity, axis=3)], axis=3
        ).astype(jnp.bfloat16)
        returned = to_latitudes(synthesis)
        scaled = returned * amplitude[None, None, :, None]
        synth_field = jnp.einsum(
            "icmj,kcm->ijk", scaled, cos_sin, preferred_element_type=jnp.float32
        ) * (1.0 / NLON)
        padded = with_halo(lat_rows, ((("band", "lon"), 1),), 1).astype(jnp.float32)
        rates_f32 = lat_rows.astype(jnp.float32)
        lateral_term = (
            jnp.roll(rates_f32, 1, axis=2)
            + jnp.roll(rates_f32, -1, axis=2)
            + padded[:, 2:, :]
            + padded[:, :-2, :]
            - 4.0 * rates_f32
        )
        coupled = synth_field + lateral[:, None, None] * lateral_term
        coupled_grid = lax.all_to_all(
            coupled.astype(jnp.bfloat16), "lon", split_axis=2, concat_axis=1, tiled=True
        ).astype(coupled.dtype)
        forcing = -decay_row[:, None, None] * activity_now + coupled_grid + drive_f32
        activity_now = activity_now + time_step * forcing
    return activity_now


MESH = pl.DeviceIdType.MESH
LANES = 128


def remote(src, dst, send_sem, recv_sem, peer):
    return pltpu.make_async_remote_copy(
        src_ref=src, dst_ref=dst, send_sem=send_sem, recv_sem=recv_sem,
        device_id=peer, device_id_type=MESH,
    )


def step_kernel(nband, t_ref, mirror_ref, mirrors_ref, w_ref, b_hbm, a_ref, k_ref,
                u_ref, drive_ref, par_ref, un_ref, *rest):
    (rates_ref, face_ref, ps_ref, pr_ref, fz_ref, gz_ref, b_ref, own_ref, other_ref, x_ref, y_ref, s_ref, o_ref,
     field_ref, pad_ref, edge_ref, around_ref, af_ref, col_ref, side_ref, we_ref,
     bsem, ps, pr, zs, zr, ss, rs, ys, yr, xs, xr, es, er) = rest
    band, lon = lax.axis_index("band"), lax.axis_index("lon")
    rows, nlon = rates_ref.shape
    owned, half_lat, deg = b_ref.shape
    groups = t_ref.shape[0]
    group = owned // groups
    half = own_ref.shape[1]
    both = 2 * half
    npop = half // 2
    hb = nband // 2
    nlat = half_lat // hb
    lines = 2 * group
    first = (band * lax.axis_size("lon") + lon) * owned
    kinds = k_ref.shape[0]
    across = {"lon": 1 - lon}
    mate = {"pop": 1 - lax.axis_index("pop")}
    tiles = x_ref.shape[0]
    spare = tiles * LANES - half_lat
    padding = [jnp.zeros((group, spare), jnp.float32)] if spare else []
    wide_padding = [jnp.zeros((both, spare), jnp.float32)] if spare else []
    degree = lax.broadcasted_iota(jnp.int32, (half, deg), 1)
    along = (((1,), (1,)), ((), ()))
    down = (((0,), (0,)), ((), ()))

    def forward_band(d):
        return lax.rem(band + d, nband)

    def backward_band(d):
        return lax.rem(band + nband - d, nband)

    def fetch(g):
        part = pl.ds(g * group, group)
        return pltpu.make_async_copy(b_hbm.at[part], b_ref.at[part], bsem.at[g])

    def partial(g):
        return remote(ps_ref.at[g], pr_ref.at[g], ps.at[g], pr.at[g], across)

    def outward(g, d):
        dest = forward_band(d)
        return remote(
            fz_ref.at[g, dest], gz_ref.at[g, band], zs.at[g, d - 1], zr.at[g, d - 1], {"band": dest}
        )

    def swap(g):
        part = pl.ds(g * group, group)
        return remote(own_ref.at[part], other_ref.at[part], ss.at[g], rs.at[g], mate)

    def homeward(g, d):
        dest = forward_band(d)
        return remote(
            s_ref.at[g, dest], o_ref.at[g, 0, band], ys.at[g, d - 1], yr.at[g, d - 1], {"band": dest}
        )

    def cross(g, d):
        source = backward_band(d)
        block = s_ref.at[g, band] if d == 0 else o_ref.at[g, 0, source]
        return remote(block, o_ref.at[g, 1, source], xs.at[g, d], xr.at[g, d], across)

    def edge(side):
        peer = {"band": forward_band(1 if side == 0 else nband - 1)}
        return remote(edge_ref.at[side], around_ref.at[side], es.at[side], er.at[side], peer)

    def column():
        return remote(col_ref, side_ref, es.at[2], er.at[2], across)

    @pl.loop(0, groups)
    def _(g):
        fetch(g).start()

    barrier = pltpu.get_barrier_semaphore()
    for d in range(1, nband):
        peer = {"band": forward_band(d)}
        pl.semaphore_signal(barrier, inc=1, device_id=peer, device_id_type=MESH)
    pl.semaphore_signal(barrier, inc=1, device_id=across, device_id_type=MESH)
    pl.semaphore_signal(barrier, inc=1, device_id=mate, device_id_type=MESH)

    @pl.loop(0, npop)
    def _(i):
        gain, thresh = par_ref[0, i], par_ref[1, i]
        for r in range(0, nlat, 16):
            here = pl.ds(pl.multiple_of(i * nlat + r, 16), 16)
            rates_ref[here] = jax.nn.sigmoid(gain * (u_ref[here] - thresh)).astype(rates_ref.dtype)
        part = pl.ds(pl.multiple_of(i * nlat, 16), nlat)
        face_ref[part] = jnp.dot(
            mirror_ref[...], rates_ref[part], preferred_element_type=jnp.float32
        ).astype(face_ref.dtype)
    pl.semaphore_wait(barrier, nband + 1)

    @pl.loop(0, groups)
    def _(g):
        ps_ref[g] = lax.dot_general(
            t_ref[g, 1], face_ref[...], along, preferred_element_type=jnp.float32
        ).astype(ps_ref.dtype)
        partial(g).start()

    fill = jnp.zeros((16 - npop, nlon), jnp.float32)
    for side, at in ((0, nlat - 1), (1, 0)):
        picked = [
            rates_ref[i * nlat + at : i * nlat + at + 1].astype(jnp.float32) for i in range(npop)
        ]
        edge_ref[side] = jnp.concatenate(picked + [fill], axis=0).astype(edge_ref.dtype)
    r16 = lax.broadcasted_iota(jnp.int32, (16, nlon), 0)
    c16 = lax.broadcasted_iota(jnp.int32, (16, nlon), 1)
    pick = ((r16 == 0) & (c16 == nlon - 1)) | ((r16 == 1) & (c16 == 0))
    col_ref[...] = lax.dot_general(
        jnp.where(pick, 1.0, 0.0).astype(jnp.bfloat16), rates_ref[...], along,
        preferred_element_type=jnp.float32,
    ).astype(col_ref.dtype)
    edge(0).start()
    edge(1).start()
    column().start()
    field_ref[...] = jnp.zeros_like(field_ref)

    def analyse_longitudes(g):
        total = lax.dot_general(
            t_ref[g, 0], face_ref[...], along, preferred_element_type=jnp.float32
        )
        partial(g).wait_recv()
        total = (total + pr_ref[g].astype(jnp.float32)).astype(fz_ref.dtype)
        fz_ref[g] = total.reshape(fz_ref.shape[1:])
        for d in range(1, nband):
            outward(g, d).start()
        gz_ref[g, band] = fz_ref[g, band]

    def analyse_latitudes(g):
        for d in range(1, nband):
            outward(g, d).wait_recv()
        for cc in range(2):
            part = slice(cc * group, (cc + 1) * group)
            parts = []
            for h in range(hb):
                north = gz_ref[g, h, part, :].astype(jnp.float32)
                south = gz_ref[g, nband - 1 - h, part, :].astype(jnp.float32)
                parts.append((w_ref[h] * (north + south), w_ref[h] * (north - south)))
            for side in range(2):
                for i in range(npop):
                    row = side * half + i * 2 + cc
                    line = [piece[side][:, i * nlat : (i + 1) * nlat] for piece in parts]
                    line = jnp.concatenate(line + padding, axis=1)
                    for t in range(tiles):
                        x_ref[t, pl.ds(row, group, stride=both), :] = line[
                            :, t * LANES : (t + 1) * LANES
                        ]
        fetch(g).wait()
        for k in range(group):
            m = g * group + k
            x = [x_ref[t, k * both : (k + 1) * both, :] for t in range(tiles)]
            x = jnp.concatenate(x, axis=1)[:, :half_lat].astype(jnp.bfloat16)
            parity = jnp.dot(x, b_ref[m], preferred_element_type=jnp.float32)
            gap = degree - (first + m)
            coeffs = jnp.where((gap & 1) == 0, parity[:half], parity[half:])
            own_ref[m] = jnp.where(gap >= 0, coeffs, 0.0).astype(own_ref.dtype)
        swap(g).start()

    def synthesise(g):
        swap(g).wait_recv()
        for k in range(group):
            m = g * group + k
            pair = jnp.concatenate(
                [own_ref[m].astype(jnp.float32), other_ref[m].astype(jnp.float32)], axis=0
            ).astype(jnp.bfloat16)
            by_kind = jnp.dot(
                a_ref[...], jnp.concatenate([pair, pair], axis=0),
                preferred_element_type=jnp.float32,
            )
            mixed = k_ref[0:1] * by_kind[:half]
            for kind in range(1, kinds):
                mixed += k_ref[kind : kind + 1] * by_kind[kind * half : (kind + 1) * half]
            gap = degree - (first + m)
            signed = jnp.where((gap & 1) == 0, mixed, -mixed)
            y = lax.dot_general(
                jnp.concatenate([mixed, signed], axis=0).astype(jnp.bfloat16), b_ref[m],
                along, preferred_element_type=jnp.float32,
            )
            y = y * jnp.where(first + m == 0, 1.0, 2.0)
            y = jnp.concatenate([y] + wide_padding, axis=1)
            for t in range(tiles):
                y_ref[t, k * both : (k + 1) * both, :] = y[:, t * LANES : (t + 1) * LANES]
        for side in range(2):
            blocks = [[None, None] for h in range(hb)]
            for cc in range(2):
                wide = [
                    jnp.concatenate(
                        [
                            y_ref[t, pl.ds(side * half + i * 2 + cc, group, stride=both), :]
                            for t in range(tiles)
                        ],
                        axis=1,
                    )
                    for i in range(npop)
                ]
                for h in range(hb):
                    blocks[h][cc] = jnp.concatenate(
                        [row[:, h * nlat : (h + 1) * nlat] for row in wide], axis=1
                    ).astype(s_ref.dtype)
            joined = jnp.concatenate([piece for block in blocks for piece in block], axis=0)
            if side == 1:
                joined = jnp.dot(
                    joined, mirrors_ref[...], preferred_element_type=jnp.float32
                ).astype(s_ref.dtype)
            for h in range(hb):
                dest = h if side == 0 else nband - 1 - h
                s_ref[g, dest] = joined[h * lines : (h + 1) * lines]
        for d in range(1, nband):
            homeward(g, d).start()
        cross(g, 0).start()
        o_ref[g, 0, band] = s_ref[g, band]

    def pass_on(g):
        for d in range(1, nband):
            homeward(g, d).wait_recv()
            cross(g, d).start()

    def synthesise_longitudes(g):
        for d in range(nband):
            cross(g, d).wait_recv()
        waves = 2 * nband * lines
        table = t_ref[g].reshape(waves, nlon)
        for q in range(0, rows, LANES):
            field_ref[q : q + LANES] += lax.dot_general(
                o_ref[g, :, :, :, q : q + LANES].reshape(waves, LANES), table, down,
                preferred_element_type=jnp.float32,
            )

    stages = (analyse_longitudes, analyse_latitudes, synthesise, pass_on, synthesise_longitudes)

    @pl.loop(0, groups + len(stages) - 1)
    def _(t):
        for late, stage in enumerate(stages):
            @pl.when((t >= late) & (t < groups + late))
            def _():
                stage(t - late)

    edge(0).wait_recv()
    edge(1).wait_recv()
    column().wait_recv()
    af_ref[...] = around_ref[...].astype(jnp.float32)
    r16 = lax.broadcasted_iota(jnp.int32, (16, LANES), 0)
    c16 = lax.broadcasted_iota(jnp.int32, (16, LANES), 1)
    place = ((r16 == 0) & (c16 == LANES - 1)) | ((r16 == 1) & (c16 == 0))
    we_ref[...] = lax.dot_general(
        side_ref[...], jnp.where(place, 1.0, 0.0).astype(jnp.bfloat16), down,
        preferred_element_type=jnp.float32,
    )
    step = 16
    scale = 1.0 / (2 * nlon)
    at = lax.broadcasted_iota(jnp.int32, (step, nlon), 1)

    @pl.loop(0, npop)
    def _(i):
        decay, lateral = par_ref[2, i], par_ref[3, i]
        base = pl.multiple_of(i * nlat, step)
        pad_ref[pl.ds(8, nlat)] = rates_ref[pl.ds(base, nlat)].astype(jnp.float32)
        pad_ref[7:8] = jnp.where(band > 0, af_ref[0, pl.ds(i, 1)], 0.0)
        pad_ref[8 + nlat : 9 + nlat] = jnp.where(band < nband - 1, af_ref[1, pl.ds(i, 1)], 0.0)
        for r in range(0, nlat, step):
            here = pl.ds(base + r, step)
            own = pad_ref[8 + r : 8 + r + step]
            ends = we_ref[here]
            beside = (
                jnp.where(at == 0, ends[:, LANES - 1 :], pltpu.roll(own, 1, 1))
                + jnp.where(at == nlon - 1, ends[:, :1], pltpu.roll(own, nlon - 1, 1))
                + pad_ref[9 + r : 9 + r + step]
                + pad_ref[7 + r : 7 + r + step]
                - 4.0 * own
            )
            u = u_ref[here]
            forcing = (
                -decay * u + field_ref[here] * scale + lateral * beside
                + drive_ref[here].astype(jnp.float32)
            )
            un_ref[here] = u + time_step * forcing

    edge(0).wait_send()
    edge(1).wait_send()
    column().wait_send()

    @pl.loop(0, groups)
    def _(g):
        partial(g).wait_send()
        swap(g).wait_send()
        for d in range(1, nband):
            outward(g, d).wait_send()
            homeward(g, d).wait_send()
        for d in range(nband):
            cross(g, d).wait_send()


def one_step(table, mirror, mirrors, weights, basis, by_kind, kernels, u, drive, params,
             nband, npop, last):
    rows, nlon = u.shape
    owned, half_lat, deg = basis.shape
    nlat = rows // npop
    groups = table.shape[0]
    group = owned // groups
    half = 2 * npop
    tiles = pl.cdiv(half_lat, LANES)
    dma = pltpu.SemaphoreType.DMA
    vmem = pl.BlockSpec(memory_space=pltpu.VMEM)
    hbm = pl.BlockSpec(memory_space=pltpu.MemorySpace.HBM)
    bf16 = jnp.bfloat16
    blocks = (groups, nband, 2 * group, rows)
    waves = nband * 2 * group
    return pl.pallas_call(
        functools.partial(step_kernel, nband),
        out_shape=jax.ShapeDtypeStruct(u.shape, jnp.float32),
        in_specs=[vmem] * 4 + [hbm] + [vmem] * 4 + [pl.BlockSpec(memory_space=pltpu.SMEM)],
        out_specs=vmem,
        scratch_shapes=[
            pltpu.VMEM((rows, nlon), bf16),
            pltpu.VMEM((rows, nlon), bf16),
            pltpu.VMEM((groups, waves, rows), bf16),
            pltpu.VMEM((groups, waves, rows), bf16),
            pltpu.VMEM(blocks, bf16),
            pltpu.VMEM(blocks, bf16),
            pltpu.VMEM(basis.shape, bf16),
            pltpu.VMEM((owned, half, deg), bf16),
            pltpu.VMEM((owned, half, deg), bf16),
            pltpu.VMEM((tiles, group * 2 * half, LANES), jnp.float32),
            pltpu.VMEM((tiles, group * 2 * half, LANES), jnp.float32),
            pltpu.VMEM(blocks, bf16),
            pltpu.VMEM((groups, 2) + blocks[1:], bf16),
            pltpu.VMEM((rows, nlon), jnp.float32),
            pltpu.VMEM((nlat + 16, nlon), jnp.float32),
            pltpu.VMEM((2, 16, nlon), bf16),
            pltpu.VMEM((2, 16, nlon), bf16),
            pltpu.VMEM((2, 16, nlon), jnp.float32),
            pltpu.VMEM((16, rows), bf16),
            pltpu.VMEM((16, rows), bf16),
            pltpu.VMEM((rows, LANES), jnp.float32),
            dma((groups,)),
            dma((groups,)), dma((groups,)),
            dma((groups, nband - 1)), dma((groups, nband - 1)),
            dma((groups,)), dma((groups,)),
            dma((groups, nband - 1)), dma((groups, nband - 1)),
            dma((groups, nband)), dma((groups, nband)),
            dma((3,)), dma((3,)),
        ],
        compiler_params=pltpu.CompilerParams(
            collective_id=1 if last else 0, has_side_effects=True, vmem_limit_bytes=60 * 2**20
        ),
        name="last_step" if last else "one_step",
    )(table, mirror, mirrors, weights, basis, by_kind, kernels, u, drive, params)


def wave_table(starts, owned, longitude, period):
    coarse = starts[:, None] + 16 * jnp.arange(owned // 16, dtype=jnp.int32)[None, :]
    fine = jnp.arange(16, dtype=jnp.int32)

    def angles(wave):
        phase = wave[..., None] * longitude % period
        angle = phase.astype(jnp.float32) * (2.0 * math.pi / period)
        return lax.optimization_barrier((jnp.cos(angle), jnp.sin(angle)))

    cos_a, sin_a = (v[:, :, None, :] for v in angles(coarse))
    cos_b, sin_b = (v[None, None, :, :] for v in angles(fine))
    shape = (starts.shape[0], owned, longitude.shape[0])
    cosine = (cos_a * cos_b - sin_a * sin_b).reshape(shape)
    sine = (sin_a * cos_b + cos_a * sin_b).reshape(shape)
    return jnp.stack([cosine, sine], axis=1)


def fast_local(activity, drive, basis, kernels, conn_block, coupling, rate_params):
    npop, nlat, nlon = activity.shape
    owned, half_lat, deg = basis.shape
    nband = lax.axis_size("band")
    hb = nband // 2
    period = nlon * lax.axis_size("lon")
    rows = npop * nlat
    band, lon, pop = lax.axis_index("band"), lax.axis_index("lon"), lax.axis_index("pop")
    pop_first = pop * npop
    params = lax.dynamic_slice_in_dim(rate_params, pop_first, npop, 1)

    bands = jnp.arange(nband, dtype=jnp.int32)
    kk = jnp.arange(nlon, dtype=jnp.int32)
    own_start = (bands * 2 + lon) * owned
    other_start = (bands * 2 + 1 - lon) * owned
    starts = jnp.concatenate([own_start, other_start])
    table = wave_table(starts, owned, lon * nlon + kk, period).astype(jnp.bfloat16)
    table = table.reshape(2, nband, 2, owned // 16, 16, nlon).transpose(3, 0, 1, 2, 4, 5)
    table = table.reshape(owned // 16, 2, nband * 32, nlon)

    row_index = jnp.arange(half_lat, dtype=jnp.float32)
    colatitude = math.pi * (4.0 * row_index + 3.0) / (8.0 * half_lat + 2.0)
    weights = math.pi * jnp.sin(colatitude) / (2.0 * half_lat)
    weights = jnp.tile(weights.reshape(hb, 1, nlat), (1, 1, npop))

    south = band >= hb
    lat = jnp.arange(nlat, dtype=jnp.int32)
    mirror = (lat[:, None] == jnp.where(south, nlat - 1 - lat, lat)[None, :]).astype(jnp.bfloat16)
    cell = jnp.arange(rows, dtype=jnp.int32)
    image = cell // nlat * nlat + (nlat - 1 - cell % nlat)
    mirrors = (cell[:, None] == image[None, :]).astype(jnp.bfloat16)

    coup_own = lax.dynamic_slice_in_dim(coupling, pop_first, npop, 0)
    block_own = lax.dynamic_slice_in_dim(conn_block, pop_first, npop, 0)
    kind = jnp.arange(kernels.shape[0], dtype=jnp.int32)
    per_kind = jnp.where(block_own[None] == kind[:, None, None], coup_own[None], 0.0)
    per_kind = jnp.concatenate(
        [
            lax.dynamic_slice_in_dim(per_kind, pop_first, npop, 2),
            lax.dynamic_slice_in_dim(per_kind, (1 - pop) * npop, npop, 2),
        ],
        axis=2,
    )
    spread = per_kind[:, :, None, :, None] * jnp.eye(2, dtype=jnp.float32)[:, None, :]
    spread = spread.reshape(kernels.shape[0] * npop * 2, 2 * npop * 2)
    coarse = lax.reduce_precision(spread, 8, 7)
    by_kind = jnp.concatenate([coarse, spread - coarse], axis=1).astype(jnp.bfloat16)

    drive = drive.reshape(rows, nlon)
    u = activity.reshape(rows, nlon)
    for step_index in range(STEPS):
        u = one_step(
            table, mirror, mirrors, weights, basis, by_kind, kernels, u, drive, params,
            nband, npop, step_index == STEPS - 1,
        )
    return u.reshape(npop, nlat, nlon)


def dispatch(activity, drive, basis, *rest):
    npop, nlat, nlon = activity.shape
    owned, half_lat, deg = basis.shape
    fits = (
        lax.axis_size("lon") == 2
        and lax.axis_size("pop") == 2
        and lax.axis_size("band") % 2 == 0
        and npop == 4
        and owned % 16 == 0
        and nlat % 16 == 0
        and (npop * nlat) % LANES == 0
        and nlon % LANES == 0
        and deg % LANES == 0
        and 2 * basis.size <= 40 * 2**20
    )
    return (fast_local if fits else local)(activity, drive, basis, *rest)


def solution(mesh):
    in_specs = (
        P(("subj", "pop"), "band", "lon"),
        P(("subj", "pop"), "band", "lon"),
        P(("subj", "band", "lon"), None, None),
        P(),
        P(),
        P("subj", None),
        P("subj", None),
    )
    out_specs = P(("subj", "pop"), "band", "lon")
    return jax.shard_map(
        dispatch, mesh=mesh, in_specs=in_specs, out_specs=out_specs, check_vma=False
    )
```
